1024 devices in a mesh: lat: 16 (over x, core), lon: 64 (over z, y).
Axes of the slice: x: 8, y: 8, z: 8, core: 2. Of those that a mesh axis runs over, the one named last changes fastest.
Arguments:
- eastward_velocity: float32 [384, 1024, 128], P('lat', 'lon'), may hold values from -6 to 6
- northward_velocity: float32 [384, 1024, 128], P('lat', 'lon'), may hold values from -6 to 6
- thermal_anomaly: float32 [384, 1024, 128], P('lat', 'lon'), may hold values from -6 to 6
- water_content: float32 [384, 1024, 128], P('lat', 'lon'), may hold values from 0 to 1
- gridbox_factor: float32 [384, 1024], replicated, may hold values from 0.5 to 2
- filter_threshold: float32 [384], replicated, may hold values from 0.03 to 1
- layers_to_eigen: float32 [128, 128], replicated, may hold values from -0.5 to 0.5
- eigen_to_layers: float32 [128, 128], replicated, may hold values from -0.5 to 0.5
- eigen_screening_factor: float32 [128], replicated, may hold values from 0.3 to 30
- chebyshev_sweeps: int32 [128], replicated, may hold values from 3 to 6, as said below
- eigen_region_holder: int32 [128], replicated, may hold values from 0 to 63, as said below
Outputs:
- wind_u_new: float32 [384, 1024, 128], P('lat', 'lon')
- wind_v_new: float32 [384, 1024, 128], P('lat', 'lon')
- mode_solution: float32 [384, 384, 1024], P('lon', 'lat')
The draws below stay inside these ranges and needn't reach their ends.
Inputs may be any that keep to these rules, and one draw needn't show every extreme that they name: `chebyshev_sweeps`: some mode takes exactly 6 iterations and some exactly 3. `eigen_region_holder`: no longitude patch owns more than 6 modes, and some patch owns exactly 6.
All inputs are finite; a program needn't handle non-finite values.
Results may differ from the reference program's by a relative error of at most 0.0003.
Values sent between devices are 32-bit elements; how exact they have to be, the bound alone decides.
No kernel may reach another device: no remote copies, remote signals or barrier semaphores. Data moves between devices by JAX's collectives and lax.ppermute only.
A program may use at most 64 MiB of HBM per device.

```python
import math
import jax
import jax.numpy as jnp
from jax import lax

LAYER_COUNT = 128
MAXIT = 6
PARALLEL_COUNT = 384
MERIDIAN_COUNT = 1024
PATCHES = 64
MAXM = 6
SLOTS = 384


def draw_chebyshev_sweeps(key, part):
    first_key, second_key = jax.random.split(jax.random.fold_in(key, 11))
    base = jax.random.randint(first_key, (LAYER_COUNT,), 3, MAXIT + 1)
    chosen = jax.random.randint(second_key, (), 0, LAYER_COUNT)
    mode_index = jnp.arange(LAYER_COUNT)
    base = jnp.where(mode_index == chosen, MAXIT, base)
    base = jnp.where(mode_index == (chosen + 1) % LAYER_COUNT, 3, base)
    return base.astype(jnp.int32)


def draw_eigen_region_holder(key, part):
    owner_keys = jax.random.split(jax.random.fold_in(key, 23), 3)
    heavy = jax.random.randint(owner_keys[0], (), 0, PATCHES)
    others = jax.random.permutation(owner_keys[1], (PATCHES - 1) * MAXM)[:LAYER_COUNT - MAXM] // MAXM
    others = others + (others >= heavy).astype(jnp.int32)
    table = jnp.concatenate([jnp.zeros((MAXM,), jnp.int32) + heavy, others.astype(jnp.int32)])
    order = jax.random.permutation(owner_keys[2], LAYER_COUNT)
    return table[order].astype(jnp.int32)


def block_levels(own_key, extent, pieces, smallest, largest):
    factor_of, own = 1.0, jax.random.fold_in(own_key, 6)
    for dim, parts in pieces:
        heights = jnp.exp(jax.random.uniform(jax.random.fold_in(own, dim), (parts,), jnp.float32, smallest / len(pieces), largest / len(pieces)))
        factor_of = factor_of * jnp.repeat(heights, extent[dim] // parts).reshape([-1 if axis == dim else 1 for axis in range(len(extent))])
    return factor_of


def gaussian(rng, shape, deviation, most, shards=(), held_as=jnp.bfloat16):
    array = deviation * jax.random.normal(rng, shape, jnp.float32)
    if shards:
        array = array * block_levels(rng, shape, shards, -0.22, 0.18)
    return jnp.clip(array, -most, most).astype(held_as)


def setup_inputs(seed: int = 0) -> dict:
    key_of = jax.random.split(jax.random.key(seed), 12)
    return {
        "eastward_velocity": gaussian(key_of[0], (PARALLEL_COUNT, MERIDIAN_COUNT, LAYER_COUNT), 1.0, 6.0, ((0, 16), (1, 64)), jnp.float32),
        "northward_velocity": gaussian(key_of[1], (PARALLEL_COUNT, MERIDIAN_COUNT, LAYER_COUNT), 1.0, 6.0, ((0, 16), (1, 64)), jnp.float32),
        "thermal_anomaly": gaussian(key_of[2], (PARALLEL_COUNT, MERIDIAN_COUNT, LAYER_COUNT), 1.0, 6.0, ((0, 16), (1, 64)), jnp.float32),
        "water_content": jnp.clip(1.0 * jax.random.uniform(key_of[3], (PARALLEL_COUNT, MERIDIAN_COUNT, LAYER_COUNT), jnp.float32) ** block_levels(key_of[3], (PARALLEL_COUNT, MERIDIAN_COUNT, LAYER_COUNT), ((0, 16), (1, 64)), -0.2, 0.2), 0.0, 1.0),
        "gridbox_factor": jnp.clip(jnp.exp(jax.random.uniform(key_of[4], (PARALLEL_COUNT, MERIDIAN_COUNT), jnp.float32, math.log(0.5), math.log(2.0))), 0.5, 2.0),
        "filter_threshold": jnp.clip(jnp.exp(jax.random.uniform(key_of[5], (PARALLEL_COUNT,), jnp.float32, math.log(0.03), math.log(1.0))), 0.03, 1.0),
        "layers_to_eigen": gaussian(key_of[6], (LAYER_COUNT, LAYER_COUNT), LAYER_COUNT ** -0.5, 0.5, (), jnp.float32),
        "eigen_to_layers": gaussian(key_of[7], (LAYER_COUNT, LAYER_COUNT), LAYER_COUNT ** -0.5, 0.5, (), jnp.float32),
        "eigen_screening_factor": jnp.clip(jnp.exp(jax.random.uniform(key_of[8], (LAYER_COUNT,), jnp.float32, math.log(0.3), math.log(30.0))), 0.3, 30.0),
        "chebyshev_sweeps": draw_chebyshev_sweeps(jax.random.fold_in(key_of[11], 71), 0),
        "eigen_region_holder": draw_eigen_region_holder(jax.random.fold_in(key_of[11], 71), 0),
    }


highest = lax.Precision.HIGHEST
viscous_factor = 0.125
elastic_factor = 0.5
step_coef = 0.5
moisture_factor = 0.61


def northward_offset(values, offset):
    zeros_row = jnp.zeros_like(values[:1])
    if offset == 1:
        return jnp.concatenate([values[1:], zeros_row], axis=0)
    return jnp.concatenate([zeros_row, values[:-1]], axis=0)


def eastward_offset(values, offset):
    return jnp.roll(values, -offset, axis=1)


def apply_helm(values, gridbox_factor, depth_value):
    adjacent_regions = northward_offset(values, 1) + northward_offset(values, -1) + eastward_offset(values, 1) + eastward_offset(values, -1)
    return values - depth_value * gridbox_factor * (adjacent_regions - 4.0 * values)


def chebyshev(source, gridbox_factor, depth_value, count_value):
    centre = 1.0 + 8.0 * depth_value
    radius = 8.0 * depth_value
    relative = centre / radius
    ratio_now = 1.0 / relative
    direction = source / centre
    residual = source
    solution = jnp.zeros_like(source)
    for sweep in range(MAXIT):
        active = jnp.where(count_value > sweep, 1.0, 0.0).astype(jnp.float32)
        solution = solution + active * direction
        if sweep + 1 < MAXIT:
            residual = residual - apply_helm(direction, gridbox_factor, depth_value)
            ratio_next = 1.0 / (2.0 * relative - ratio_now)
            direction = ratio_next * ratio_now * direction + (2.0 * ratio_next / radius) * residual
            ratio_now = ratio_next
    return solution


def damp_factor(cutoff_rows, lon_total, folded):
    scale = cutoff_rows[:, None] * (0.5 * lon_total)
    ratio = folded[None, :] / scale
    ratio = ratio * ratio
    return 1.0 / (1.0 + ratio * ratio)


def polar_filter(grid_field, filter_threshold):
    lon_total = grid_field.shape[1]
    wavenumber = jnp.arange(lon_total)
    folded = jnp.minimum(wavenumber, lon_total - wavenumber).astype(jnp.float32)
    damping = damp_factor(filter_threshold, lon_total, folded)
    spectrum = jnp.fft.fft(grid_field, axis=1)
    return jnp.real(jnp.fft.ifft(spectrum * damping, axis=1)).astype(jnp.float32)


def reference(eastward_velocity, northward_velocity, thermal_anomaly, water_content, gridbox_factor, filter_threshold, layers_to_eigen, eigen_to_layers, eigen_screening_factor, chebyshev_sweeps, eigen_region_holder):
    moist_thermal_field = thermal_anomaly * (1.0 + moisture_factor * water_content)
    gridbox_scaling = gridbox_factor[:, :, None]
    outflow_field = gridbox_scaling * ((eastward_offset(eastward_velocity, 1) - eastward_offset(eastward_velocity, -1)) + (northward_offset(northward_velocity, 1) - northward_offset(northward_velocity, -1))) * 0.5
    adjacent_regions = northward_offset(moist_thermal_field, 1) + northward_offset(moist_thermal_field, -1) + eastward_offset(moist_thermal_field, 1) + eastward_offset(moist_thermal_field, -1)
    source_term = moist_thermal_field + viscous_factor * gridbox_scaling * (adjacent_regions - 4.0 * moist_thermal_field) - elastic_factor * outflow_field
    mode_rhs = jnp.einsum('abk,mk->mab', source_term, layers_to_eigen, precision=highest)

    def solve_one(item):
        source, depth_value, count_value = item
        return polar_filter(chebyshev(source, gridbox_factor, depth_value, count_value), filter_threshold)

    potential = lax.map(solve_one, (mode_rhs, eigen_screening_factor, chebyshev_sweeps))
    mode_index = jnp.arange(LAYER_COUNT)
    earlier = jnp.logical_and(eigen_region_holder[:, None] == eigen_region_holder[None, :], mode_index[:, None] > mode_index[None, :])
    slot_rank = jnp.sum(earlier.astype(jnp.int32), axis=1)
    position = (eigen_region_holder * MAXM + slot_rank).astype(jnp.int32)
    mode_solution = jnp.zeros((SLOTS, PARALLEL_COUNT, MERIDIAN_COUNT), jnp.float32).at[position].set(potential)
    pressure = jnp.einsum('mab,km->abk', potential, eigen_to_layers, precision=highest)
    grad_lon = gridbox_scaling * (eastward_offset(pressure, 1) - eastward_offset(pressure, -1)) * 0.5
    grad_lat = gridbox_scaling * (northward_offset(pressure, 1) - northward_offset(pressure, -1)) * 0.5
    return (eastward_velocity - step_coef * grad_lon, northward_velocity - step_coef * grad_lat, mode_solution)
```

```python
import math

import jax
import jax.numpy as jnp
import numpy as np
from jax import lax
from jax.experimental import pallas as pl
from jax.experimental.pallas import tpu as pltpu
from jax.sharding import PartitionSpec as P

MAXIT = 6
ROWS = 24
COLS = 16
CELLS = ROWS * COLS
LON = 1024
LAT = 384
MODES = 128
PATCHES = 64
SLOTS = 6
HOST = 2
EXT = 40
BLOCKS = LON // 128

f32 = jnp.float32
bf16 = jnp.bfloat16
VMEM = pl.BlockSpec(memory_space=pltpu.VMEM)
ANY = pl.BlockSpec(memory_space=pl.ANY)


def filter_tables():
    b = np.arange(128)[:, None].astype(np.float64)
    table = np.zeros((4, 256, 256))
    wave = np.zeros((4, 256))
    gain = np.zeros((4, 256))
    k2 = np.arange(65)[None, :]
    angle = 2 * np.pi * b * k2 / 128
    table[0, :128, :65] = np.cos(angle)
    table[0, :128, 65:128] = np.sin(angle[:, 1:64])
    wave[0, :65] = 8 * np.arange(65)
    wave[0, 65:128] = 8 * np.arange(1, 64)
    gain[0, :128] = 2.0
    gain[0, 0] = gain[0, 64] = 1.0
    k2 = np.arange(64)[None, :]
    angle = 2 * np.pi * b * (4 + 8 * k2) / 1024
    table[0, 128:, 128:192] = np.cos(angle)
    table[0, 128:, 192:] = np.sin(angle)
    wave[0, 128:192] = wave[0, 192:] = 4 + 8 * np.arange(64)
    gain[0, 128:] = 2.0
    for k1 in (1, 2, 3):
        k = k1 + 8 * np.arange(128)
        angle = 2 * np.pi * b * k[None, :] / 1024
        c, s = np.cos(angle), np.sin(angle)
        table[k1, :128, :128] = c
        table[k1, :128, 128:] = -s
        table[k1, 128:, :128] = s
        table[k1, 128:, 128:] = c
        wave[k1, :128] = wave[k1, 128:] = np.minimum(k, 1024 - k)
        gain[k1] = 2.0
    return table, wave, gain / LON


def split_value(x):
    high = x.astype(bf16)
    low = (x - high.astype(f32)).astype(bf16)
    return high, low


def dot3(a, b, dims):
    ah, al = a
    bh, bl = b

    def dot(x, y):
        return lax.dot_general(x, y, (dims, ((), ())), preferred_element_type=f32)

    return dot(ah, bh) + (dot(ah, bl) + dot(al, bh))


def block_swap(x):
    sub = lax.broadcasted_iota(jnp.int32, x.shape, 1)
    group = lax.broadcasted_iota(jnp.int32, x.shape, 2) // 16
    for d in (4, 2, 1):
        here = sub & d
        stay = here == (group & d)
        up = pltpu.roll(pltpu.roll(x, d, 1), 128 - 16 * d, 2)
        if d == 4:
            moved = up
        else:
            down = pltpu.roll(pltpu.roll(x, 8 - d, 1), 16 * d, 2)
            moved = jnp.where(here != 0, up, down)
        x = jnp.where(stay, x, moved)
    return x


def load_metric(metric, ext, sem, lat):
    start = pl.multiple_of(lat * ROWS, 8)
    low = pl.multiple_of(jnp.maximum(start - 8, 0), 8)
    high = pl.multiple_of(jnp.minimum(start + ROWS, LAT - 8), 8)
    return [
        pltpu.make_async_copy(metric.at[pl.ds(start, ROWS)], ext.at[pl.ds(8, ROWS)], sem.at[0]),
        pltpu.make_async_copy(metric.at[pl.ds(low, 8)], ext.at[pl.ds(0, 8)], sem.at[1]),
        pltpu.make_async_copy(metric.at[pl.ds(high, 8)], ext.at[pl.ds(8 + ROWS, 8)], sem.at[2]),
    ]


def mask_metric(ext, lat):
    ext[0:8, :] = ext[0:8, :] * jnp.where(lat > 0, 1.0, 0.0)
    ext[32:40, :] = ext[32:40, :] * jnp.where(lat < LAT // ROWS - 1, 1.0, 0.0)


def selection(holder):
    hb = jnp.broadcast_to(holder.astype(f32), (MODES, MODES))
    ha = hb.T
    ia = lax.broadcasted_iota(jnp.int32, (MODES, MODES), 0)
    ib = lax.broadcasted_iota(jnp.int32, (MODES, MODES), 1)
    same = jnp.where(ha == hb, 1.0, 0.0)
    before = jnp.where(ia < ib, 1.0, 0.0)
    after = jnp.where(ib < ia, 1.0, 0.0)
    rank_row = jnp.sum(same * before, axis=0, keepdims=True)
    rank_col = jnp.sum(same * after, axis=1, keepdims=True)
    over_row = jnp.where(rank_row >= HOST, 1.0, 0.0)
    over_col = jnp.where(rank_col >= HOST, 1.0, 0.0)
    over_index = jnp.sum(over_col * before, axis=0, keepdims=True)
    patch_a = (ia & (PATCHES - 1)).astype(f32)
    patch_b = (ib & (PATCHES - 1)).astype(f32)
    turn_a = (ia // PATCHES).astype(f32)
    turn_b = (ib // PATCHES).astype(f32)
    count_col = jnp.sum(jnp.where(hb == patch_a, 1.0, 0.0), axis=1, keepdims=True)
    count_row = jnp.sum(jnp.where(ha == patch_b, 1.0, 0.0), axis=0, keepdims=True)
    free_col = jnp.where(turn_a >= count_col, 1.0, 0.0)
    free_row = jnp.where(turn_b >= count_row, 1.0, 0.0)
    free_index = jnp.sum(free_row * after, axis=1, keepdims=True)
    home = jnp.where(ia.astype(f32) == rank_row * PATCHES + hb, 1.0, 0.0)
    guest = free_col * jnp.where(free_index == over_index, 1.0, 0.0)
    hosted = over_row * guest + (1.0 - over_row) * home
    rest = []
    for first in (2, 4):
        rest.append(
            jnp.where(ia.astype(f32) + first * PATCHES == rank_row * PATCHES + hb, 1.0, 0.0)
        )
    return jnp.concatenate([hosted] + rest, axis=0)


def cell_column(row):
    lane = lax.broadcasted_iota(jnp.int32, (COLS, 128), 1)
    sub = lax.broadcasted_iota(jnp.int32, (COLS, 128), 0)
    picked = jnp.where(lane == sub, jnp.broadcast_to(row, (COLS, 128)), 0.0)
    return jnp.broadcast_to(jnp.sum(picked, axis=1, keepdims=True), (COLS, 128))


def patch_kernel(
    u, v, t, q, metric, holder, project, depth, sweeps,
    packed, params, hosted, cell_metric,
    ext, own, field, chosen, sem,
):
    lat = lax.axis_index("lat")
    lon = lax.axis_index("lon")
    copies = load_metric(metric, ext, sem, lat)
    for c in copies:
        c.start()
    select = selection(holder[...])
    chosen[...] = select
    hosted[...] = select[: HOST * PATCHES].astype(bf16)
    params[...] = jnp.zeros_like(params)
    count = jnp.sum(jnp.where(holder[...] == lon, 1.0, 0.0), axis=1, keepdims=True)
    for s in range(SLOTS):
        row = chosen[pl.ds(s * PATCHES + lon, 1), :]
        value = jnp.sum(row * depth[...], axis=1, keepdims=True)
        params[0, s : s + 1, :] = jnp.broadcast_to(value, (1, 128))
        value = jnp.sum(row * sweeps[...].astype(f32), axis=1, keepdims=True)
        params[1, s : s + 1, :] = jnp.broadcast_to(value, (1, 128))
        params[2, s : s + 1, :] = jnp.broadcast_to(jnp.where(count > s, 1.0, 0.0), (1, 128))
    sel = select.astype(bf16)
    proj_high, proj_low = split_value(project[...])
    rows_high = jnp.dot(sel, proj_high, preferred_element_type=f32).astype(bf16)
    rows_low = jnp.dot(sel, proj_low, preferred_element_type=f32).astype(bf16)
    for c in copies:
        c.wait()
    mask_metric(ext, lat)

    block = lon // 8
    offset = (lon % 8) * COLS

    def lanes(b):
        return ext[:, pl.ds(pl.multiple_of(b * 128, 128), 128)]

    here = lanes(block)
    own[...] = pltpu.roll(here, (128 - offset) % 128, 1)
    west_block = jnp.where(offset == 0, (block + BLOCKS - 1) % BLOCKS, block)
    east_block = jnp.where(offset == 128 - COLS, (block + 1) % BLOCKS, block)
    west_metric = pltpu.roll(lanes(west_block), (129 - offset) % 128, 1)[8:32, 0:1]
    east_metric = pltpu.roll(lanes(east_block), (256 - COLS - offset) % 128, 1)[8:32, 0:1]

    uu = u[...].reshape(CELLS, MODES)
    vv = v[...].reshape(CELLS, MODES)
    virtual = t[...].reshape(CELLS, MODES) * (1.0 + 0.61 * q[...].reshape(CELLS, MODES))
    eighth = 0.125 * virtual
    to_west = eighth - 0.25 * uu
    to_east = eighth + 0.25 * uu
    to_south = eighth - 0.25 * vv
    to_north = eighth + 0.25 * vv
    col = lax.broadcasted_iota(jnp.int32, (CELLS, MODES), 0) & (COLS - 1)
    around = jnp.where(col == COLS - 1, 0.0, pltpu.roll(to_west, CELLS - 1, 0))
    around = around + jnp.where(col == 0, 0.0, pltpu.roll(to_east, 1, 0))
    zero = jnp.zeros((COLS, MODES), f32)
    around = around + jnp.concatenate([to_south[COLS:], zero], axis=0)
    around = around + jnp.concatenate([zero, to_north[: CELLS - COLS]], axis=0)
    scale = jnp.concatenate([cell_column(own[8 + r : 9 + r, :]) for r in range(ROWS)], axis=0)
    cell_metric[...] = 0.25 * scale
    field[0:CELLS, :] = virtual + scale * (around - 0.5 * virtual)

    field[CELLS:, :] = jnp.zeros((128, MODES), f32)
    first = t[:, 0, :] * (1.0 + 0.61 * q[:, 0, :])
    last = t[:, COLS - 1, :] * (1.0 + 0.61 * q[:, COLS - 1, :])
    edge_west = jnp.broadcast_to(west_metric, (ROWS, MODES)) * (0.125 * first - 0.25 * u[:, 0, :])
    edge_east = jnp.broadcast_to(east_metric, (ROWS, MODES)) * (
        0.125 * last + 0.25 * u[:, COLS - 1, :]
    )
    for rg in range(3):
        field[pl.ds(CELLS + rg, 8, stride=COLS), :] = edge_west[8 * rg : 8 * rg + 8]
        field[pl.ds(CELLS + 3 + rg, 8, stride=COLS), :] = edge_east[8 * rg : 8 * rg + 8]
    edge_south = cell_column(own[7:8, :]) * to_south[0:COLS]
    edge_north = cell_column(own[32:33, :]) * to_north[CELLS - COLS :]
    field[CELLS + 6 : CELLS + 16, :] = edge_north[0:10]
    field[CELLS + 22 : CELLS + 28, :] = edge_north[10:16]
    field[CELLS + 118 : CELLS + 128, :] = edge_south[0:10]
    field[CELLS + 102 : CELLS + 108, :] = edge_south[10:16]

    value = dot3((rows_high, rows_low), split_value(field[...]), ((1,), (1,)))
    for s in range(SLOTS):
        for part in range(4):
            packed[pl.ds(s * 4 + part, PATCHES, stride=4 * SLOTS), :] = value[
                s * PATCHES : (s + 1) * PATCHES, part * 128 : (part + 1) * 128
            ]


def patch_stage(u, v, t, q, metric, holder, project, depth, sweeps):
    return pl.pallas_call(
        patch_kernel,
        name="patch_stage",
        out_shape=(
            jax.ShapeDtypeStruct((PATCHES * SLOTS * 4, 128), f32),
            jax.ShapeDtypeStruct((3, 8, 128), f32),
            jax.ShapeDtypeStruct((HOST * PATCHES, MODES), bf16),
            jax.ShapeDtypeStruct((CELLS, MODES), f32),
        ),
        in_specs=[VMEM, VMEM, VMEM, VMEM, ANY, VMEM, VMEM, VMEM, VMEM],
        out_specs=(VMEM, VMEM, VMEM, VMEM),
        scratch_shapes=[
            pltpu.VMEM((EXT, LON), f32),
            pltpu.VMEM((EXT, 128), f32),
            pltpu.VMEM((CELLS + 128, MODES), f32),
            pltpu.VMEM((SLOTS * PATCHES, MODES), f32),
            pltpu.SemaphoreType.DMA((3,)),
        ],
    )(u, v, t, q, metric, holder, project, depth, sweeps)


def band_kernel(received, band, south, north):
    lane = lax.broadcasted_iota(jnp.int32, (PATCHES, 128), 1)
    place = lane & (COLS - 1)
    row = lax.broadcasted_iota(jnp.int32, (8, 128), 0)
    for s in range(SLOTS):
        edge = received[pl.ds(s * 4 + 3, PATCHES, stride=4 * SLOTS), :]
        from_east = pltpu.roll(edge, PATCHES - 1, 0)
        from_west = pltpu.roll(edge, 1, 0)
        bands = []
        for rg in range(3):
            x = received[pl.ds(s * 4 + rg, PATCHES, stride=4 * SLOTS), :]
            x = x + jnp.where(place == COLS - 1, pltpu.roll(from_east, 15 - rg, 1), 0.0)
            x = x + jnp.where(place == 0, pltpu.roll(from_west, 128 - 3 - rg, 1), 0.0)
            bands.append(block_swap(x.reshape(BLOCKS, 8, 128)))
        rim = jnp.where(
            lane < 10,
            pltpu.roll(edge, 128 - 6, 1),
            jnp.where(
                lane < 16,
                pltpu.roll(edge, 128 - 12, 1),
                jnp.where(lane < 122, pltpu.roll(edge, 128 - 6, 1), pltpu.roll(edge, 20, 1)),
            ),
        )
        rim = block_swap(rim.reshape(BLOCKS, 8, 128))
        for b in range(BLOCKS):
            at = slice(b * 128, (b + 1) * 128)
            for rg in range(3):
                band[s, 8 * rg : 8 * rg + 8, at] = bands[rg][b]
            south[s, :, at] = jnp.where(row == 7, rim[b], bands[0][b])
            north[s, :, at] = jnp.where(row == 0, rim[b], bands[2][b])


def band_stage(received):
    return pl.pallas_call(
        band_kernel,
        name="band_stage",
        out_shape=(
            jax.ShapeDtypeStruct((SLOTS, ROWS, LON), f32),
            jax.ShapeDtypeStruct((SLOTS, 8, LON), f32),
            jax.ShapeDtypeStruct((SLOTS, 8, LON), f32),
        ),
        in_specs=[VMEM],
        out_specs=(VMEM, VMEM, VMEM),
    )(received)


def solve_slots(
    first, count, band, south, north, from_south, from_north, params, cutoff, wave, gain,
    table_high, table_low, ext, spectral, solved, lat,
):
    row = lax.broadcasted_iota(jnp.int32, (8, LON), 0)
    for i in range(count):
        s = first + i
        depth = params[0, s : s + 1, 0:1]
        number = params[1, s : s + 1, 0:1]
        depth = jnp.where(depth > 0.0, depth, 1.0)
        centre = 1.0 + 8.0 * depth
        radius = 8.0 * depth
        relative = centre / radius
        ratio = 1.0 / relative

        def wide(x):
            return jnp.broadcast_to(x, (EXT, LON))

        below = from_south[s]
        above = from_north[s]
        source = jnp.concatenate(
            [
                below + jnp.where(row == 7, south[s], 0.0),
                band[s, 0:8] + jnp.where(row == 0, below, 0.0),
                band[s, 8:16],
                band[s, 16:24] + jnp.where(row == 7, above, 0.0),
                above + jnp.where(row == 0, north[s], 0.0),
            ],
            axis=0,
        )
        coupling = wide(depth) * ext[...]
        direction = source * wide(1.0 / centre)
        residual = source
        total = jnp.zeros_like(source)
        for sweep in range(MAXIT):
            total = total + wide(jnp.where(number > sweep, 1.0, 0.0)) * direction
            if sweep + 1 < MAXIT:
                around = (
                    pltpu.roll(direction, LON - 1, 1)
                    + pltpu.roll(direction, 1, 1)
                    + pltpu.roll(direction, EXT - 1, 0)
                    + pltpu.roll(direction, 1, 0)
                )
                residual = residual - direction + coupling * (around - 4.0 * direction)
                after = 1.0 / (2.0 * relative - ratio)
                direction = (
                    wide(after * ratio) * direction + wide(2.0 * after / radius) * residual
                )
                ratio = after
        x = [total[:, 128 * a : 128 * a + 128] for a in range(BLOCKS)]
        root = math.sqrt(0.5)
        s04, d04 = x[0] + x[4], x[0] - x[4]
        s26, d26 = x[2] + x[6], x[2] - x[6]
        s15, d15 = x[1] + x[5], x[1] - x[5]
        s37, d37 = x[3] + x[7], x[3] - x[7]
        even, odd = s04 + s26, s15 + s37
        lean, turn = root * (d15 - d37), root * (d15 + d37)
        at = slice(i * EXT, (i + 1) * EXT)
        spectral[0, at, 0:128] = even + odd
        spectral[0, at, 128:256] = even - odd
        spectral[1, at, 0:128] = d04 + lean
        spectral[1, at, 128:256] = -d26 - turn
        spectral[2, at, 0:128] = s04 - s26
        spectral[2, at, 128:256] = s37 - s15
        spectral[3, at, 0:128] = d04 - lean
        spectral[3, at, 128:256] = d26 - turn

    index = lax.broadcasted_iota(jnp.int32, (EXT, 128), 0) + (lat * ROWS - 8)
    lane = lax.broadcasted_iota(jnp.int32, (EXT, 128), 1)
    limit = jnp.zeros((EXT, 1), f32)
    for b in range(LAT // 128):
        picked = jnp.where(
            lane + 128 * b == index, jnp.broadcast_to(cutoff[b : b + 1, :], (EXT, 128)), 0.0
        )
        limit = limit + jnp.sum(picked, axis=1, keepdims=True)
    limit = jnp.where(limit > 0.0, limit, 1.0)
    inverse = 1.0 / (limit * (0.5 * LON))
    for k in range(4):
        table = (table_high[k], table_low[k])
        ratio = jnp.broadcast_to(wave[k : k + 1, :], (EXT, 256)) * jnp.broadcast_to(
            inverse, (EXT, 256)
        )
        ratio = ratio * ratio
        damping = jnp.broadcast_to(gain[k : k + 1, :], (EXT, 256)) / (1.0 + ratio * ratio)
        damping = jnp.concatenate([damping] * count, axis=0)
        spectrum = dot3(split_value(spectral[k, 0 : count * EXT, :]), table, ((1,), (0,)))
        spectral[k, 0 : count * EXT, :] = dot3(
            split_value(spectrum * damping), table, ((1,), (1,))
        )
    root = math.sqrt(0.5)
    y0 = spectral[0, 0 : count * EXT, 0:128]
    y4 = spectral[0, 0 : count * EXT, 128:256]
    p1, q1 = spectral[1, 0 : count * EXT, 0:128], spectral[1, 0 : count * EXT, 128:256]
    p2, q2 = spectral[2, 0 : count * EXT, 0:128], spectral[2, 0 : count * EXT, 128:256]
    p3, q3 = spectral[3, 0 : count * EXT, 0:128], spectral[3, 0 : count * EXT, 128:256]
    even, odd = y0 + y4, y0 - y4
    a1, b1 = root * p1, root * q1
    a3, b3 = root * p3, root * q3
    swing = q3 - q1
    parts = [None] * 8
    base, side = even + p2, p1 + p3
    parts[0], parts[4] = base + side, base - side
    base, side = even - p2, swing
    parts[2], parts[6] = base + side, base - side
    base, side = odd - q2, (a1 - b1) - (a3 + b3)
    parts[1], parts[5] = base + side, base - side
    base, side = odd + q2, (a3 - b3) - (a1 + b1)
    parts[3], parts[7] = base + side, base - side
    for i in range(count):
        for a in range(BLOCKS):
            solved[i, :, 128 * a : 128 * a + 128] = parts[a][i * EXT : (i + 1) * EXT]


def host_kernel(
    band, south, north, from_south, from_north, params, metric, cutoff, wave, gain,
    table_high, table_low,
    packed, own_modes,
    ext, spectral, solved, sem,
):
    lat = lax.axis_index("lat")
    copies = load_metric(metric, ext, sem, lat)
    for c in copies:
        c.start()
    for c in copies:
        c.wait()
    mask_metric(ext, lat)
    solve_slots(
        0, HOST, band, south, north, from_south, from_north, params, cutoff, wave, gain,
        table_high, table_low, ext, spectral, solved, lat,
    )
    lane = lax.broadcasted_iota(jnp.int32, (PATCHES, 128), 1)
    place = lane & (COLS - 1)
    for i in range(HOST):
        owned = jnp.broadcast_to(params[2, i : i + 1, 0:1], (ROWS, LON))
        own_modes[i] = solved[i, 8:32, :] * owned
        tiles = []
        for tile in range(5):
            x = jnp.stack(
                [solved[i, 8 * tile : 8 * tile + 8, 128 * b : 128 * b + 128] for b in range(BLOCKS)]
            )
            tiles.append(block_swap(x).reshape(PATCHES, 128))
        edge = jnp.zeros((PATCHES, 128), f32)
        for rg in range(3):
            x = tiles[rg + 1]
            packed[pl.ds(i * 4 + rg, PATCHES, stride=4 * HOST), :] = x
            west = pltpu.roll(pltpu.roll(x, 1, 0), 128 - 15 + rg, 1)
            east = pltpu.roll(pltpu.roll(x, PATCHES - 1, 0), 3 + rg, 1)
            edge = jnp.where(place == rg, west, edge)
            edge = jnp.where(place == 3 + rg, east, edge)
        far, near = tiles[4], tiles[0]
        edge = jnp.where((lane >= 6) & (lane < 16), pltpu.roll(far, 6, 1), edge)
        edge = jnp.where((lane >= 22) & (lane < 28), pltpu.roll(far, 12, 1), edge)
        edge = jnp.where(lane >= 118, pltpu.roll(near, 6, 1), edge)
        edge = jnp.where((lane >= 102) & (lane < 108), pltpu.roll(near, 108, 1), edge)
        packed[pl.ds(i * 4 + 3, PATCHES, stride=4 * HOST), :] = edge


def solver_scratch(count):
    return [
        pltpu.VMEM((EXT, LON), f32),
        pltpu.VMEM((4, count * EXT, 256), f32),
        pltpu.VMEM((count, EXT, LON), f32),
        pltpu.SemaphoreType.DMA((3,)),
    ]


def host_stage(*operands):
    return pl.pallas_call(
        host_kernel,
        name="host_stage",
        out_shape=(
            jax.ShapeDtypeStruct((PATCHES * HOST * 4, 128), f32),
            jax.ShapeDtypeStruct((HOST, ROWS, LON), f32),
        ),
        in_specs=[VMEM] * 6 + [ANY] + [VMEM] * 5,
        out_specs=(VMEM, VMEM),
        scratch_shapes=solver_scratch(HOST),
    )(*operands)


def rest_kernel(
    band, south, north, from_south, from_north, params, metric, cutoff, wave, gain,
    table_high, table_low, own_modes, hosted, expand,
    modes, expand_high, expand_low,
    ext, spectral, solved, sem,
):
    lat = lax.axis_index("lat")
    copies = load_metric(metric, ext, sem, lat)
    for c in copies:
        c.start()
    for c in copies:
        c.wait()
    mask_metric(ext, lat)
    high, low = split_value(expand[...])
    dims = (((1,), (1,)), ((), ()))
    expand_high[...] = lax.dot_general(
        hosted[...], high, dims, preferred_element_type=f32
    ).astype(bf16)
    expand_low[...] = lax.dot_general(
        hosted[...], low, dims, preferred_element_type=f32
    ).astype(bf16)
    modes[0:HOST] = own_modes[...]
    solve_slots(
        HOST, SLOTS - HOST, band, south, north, from_south, from_north, params, cutoff, wave, gain,
        table_high, table_low, ext, spectral, solved, lat,
    )
    for i in range(SLOTS - HOST):
        modes[HOST + i] = solved[i, 8:32, :]


def rest_stage(*operands):
    return pl.pallas_call(
        rest_kernel,
        name="rest_stage",
        out_shape=(
            jax.ShapeDtypeStruct((SLOTS, ROWS, LON), f32),
            jax.ShapeDtypeStruct((MODES, MODES), bf16),
            jax.ShapeDtypeStruct((MODES, MODES), bf16),
        ),
        in_specs=[VMEM] * 6 + [ANY] + [VMEM] * 8,
        out_specs=(VMEM, VMEM, VMEM),
        scratch_shapes=solver_scratch(SLOTS - HOST),
    )(*operands)


def wind_kernel(received, expand_high, expand_low, cell_metric, u, v, u_new, v_new, tall, edge):
    table = (expand_high[...], expand_low[...])
    for part in range(4):
        x = jnp.concatenate(
            [received[pl.ds(i * 4 + part, PATCHES, stride=4 * HOST), :] for i in range(HOST)],
            axis=0,
        )
        value = dot3(split_value(x.T), table, ((1,), (0,)))
        if part < 3:
            tall[COLS + part * 128 : COLS + part * 128 + 128, :] = value
        else:
            edge[...] = value
    tall[0:10, :] = edge[118:128, :]
    tall[10:16, :] = edge[102:108, :]
    tall[CELLS + COLS : CELLS + COLS + 10, :] = edge[6:16, :]
    tall[CELLS + COLS + 10 : CELLS + 2 * COLS, :] = edge[22:28, :]
    pressure = tall[COLS : CELLS + COLS, :]

    def spread(base):
        return jnp.concatenate(
            [
                jnp.broadcast_to(
                    edge[(r % 8) * COLS + base + r // 8 : (r % 8) * COLS + base + r // 8 + 1, :],
                    (COLS, MODES),
                )
                for r in range(ROWS)
            ],
            axis=0,
        )

    col = lax.broadcasted_iota(jnp.int32, (CELLS, MODES), 0) & (COLS - 1)
    east = jnp.where(col == COLS - 1, spread(3), pltpu.roll(pressure, CELLS - 1, 0))
    west = jnp.where(col == 0, spread(0), pltpu.roll(pressure, 1, 0))
    scale = cell_metric[...]
    u_new[...] = u[...] - (scale * (east - west)).reshape(ROWS, COLS, MODES)
    slope = tall[2 * COLS : CELLS + 2 * COLS, :] - tall[0:CELLS, :]
    v_new[...] = v[...] - (scale * slope).reshape(ROWS, COLS, MODES)


def wind_stage(*operands):
    shape = jax.ShapeDtypeStruct((ROWS, COLS, MODES), f32)
    return pl.pallas_call(
        wind_kernel,
        name="wind_stage",
        out_shape=(shape, shape),
        in_specs=[VMEM] * 6,
        out_specs=(VMEM, VMEM),
        scratch_shapes=[
            pltpu.VMEM((CELLS + 2 * COLS, MODES), f32),
            pltpu.VMEM((128, MODES), f32),
        ],
    )(*operands)


def exchange(x, rows):
    x = x.reshape(PATCHES, rows, 128)
    x = lax.all_to_all(x, "lon", split_axis=0, concat_axis=0, tiled=True)
    return x.reshape(PATCHES * rows, 128)


def local(
    eastward_velocity,
    northward_velocity,
    thermal_anomaly,
    water_content,
    gridbox_factor,
    filter_threshold,
    layers_to_eigen,
    eigen_to_layers,
    eigen_screening_factor,
    chebyshev_sweeps,
    eigen_region_holder,
):
    table, wave, gain = filter_tables()
    table_high = np.asarray(table, np.float32).astype(bf16)
    table_low = (table - table_high.astype(np.float64)).astype(np.float32).astype(bf16)
    table_high, table_low = jnp.asarray(table_high), jnp.asarray(table_low)
    wave, gain = jnp.asarray(wave, f32), jnp.asarray(gain, f32)
    packed, params, hosted, cell_metric = patch_stage(
        eastward_velocity,
        northward_velocity,
        thermal_anomaly,
        water_content,
        gridbox_factor,
        eigen_region_holder.reshape(1, MODES),
        layers_to_eigen,
        eigen_screening_factor.reshape(1, MODES),
        chebyshev_sweeps.reshape(1, MODES),
    )
    band, south, north = band_stage(exchange(packed, 4 * SLOTS))
    size = lax.axis_size("lat")
    up = [(i, i + 1) for i in range(size - 1)]
    down = [(j, i) for i, j in up]
    from_south = lax.ppermute(north, "lat", up)
    from_north = lax.ppermute(south, "lat", down)
    solver = (
        band, south, north, from_south, from_north, params, gridbox_factor,
        filter_threshold.reshape(LAT // 128, 128), wave, gain, table_high, table_low,
    )
    returned, own_modes = host_stage(*solver)
    returned = exchange(returned, 4 * HOST)
    mode_solution, expand_high, expand_low = rest_stage(
        *solver, own_modes, hosted, eigen_to_layers
    )
    u_new, v_new = wind_stage(
        returned, expand_high, expand_low, cell_metric, eastward_velocity, northward_velocity
    )
    return u_new, v_new, mode_solution


def solution(mesh):
    return jax.shard_map(
        local,
        mesh=mesh,
        in_specs=(P("lat", "lon", None),) * 4 + (P(),) * 7,
        out_specs=(P("lat", "lon", None), P("lat", "lon", None), P("lon", "lat", None)),
        check_vma=False,
    )
```

```python
import math

import jax
import jax.numpy as jnp
import numpy as np
from jax import lax
from jax.experimental import pallas as pl
from jax.experimental.pallas import tpu as pltpu
from jax.sharding import PartitionSpec as P

MAXIT = 6
MINIT = 3
ROWS = 24
COLS = 16
CELLS = ROWS * COLS
LON = 1024
LAT = 384
MODES = 128
PATCHES = 64
SLOTS = 6
HOST = 2
EXT = 40
BLOCKS = LON // 128

f32 = jnp.float32
bf16 = jnp.bfloat16
GRANT = pltpu.CompilerParams(vmem_limit_bytes=24 << 20)
VMEM = pl.BlockSpec(memory_space=pltpu.VMEM)
FAR = pl.BlockSpec(memory_space=pltpu.HBM)


def filter_tables():
    b = np.arange(128)[:, None].astype(np.float64)
    table = np.zeros((4, 256, 256))
    wave = np.zeros((4, 256))
    gain = np.zeros((4, 256))
    k2 = np.arange(65)[None, :]
    angle = 2 * np.pi * b * k2 / 128
    table[0, :128, :65] = np.cos(angle)
    table[0, :128, 65:128] = np.sin(angle[:, 1:64])
    wave[0, :65] = 8 * np.arange(65)
    wave[0, 65:128] = 8 * np.arange(1, 64)
    gain[0, :128] = 2.0
    gain[0, 0] = gain[0, 64] = 1.0
    k2 = np.arange(64)[None, :]
    angle = 2 * np.pi * b * (4 + 8 * k2) / 1024
    table[0, 128:, 128:192] = np.cos(angle)
    table[0, 128:, 192:] = np.sin(angle)
    wave[0, 128:192] = wave[0, 192:] = 4 + 8 * np.arange(64)
    gain[0, 128:] = 2.0
    for k1 in (1, 2, 3):
        k = k1 + 8 * np.arange(128)
        angle = 2 * np.pi * b * k[None, :] / 1024
        c, s = np.cos(angle), np.sin(angle)
        table[k1, :128, :128] = c
        table[k1, :128, 128:] = -s
        table[k1, 128:, :128] = s
        table[k1, 128:, 128:] = c
        wave[k1, :128] = wave[k1, 128:] = np.minimum(k, 1024 - k)
        gain[k1] = 2.0
    return table, wave, gain / LON


def split_value(x):
    high = x.astype(bf16)
    low = (x - high.astype(f32)).astype(bf16)
    return high, low


def dot3(a, b, dims):
    ah, al = a
    bh, bl = b

    def dot(x, y):
        return lax.dot_general(x, y, (dims, ((), ())), preferred_element_type=f32)

    return dot(ah, bh) + (dot(ah, bl) + dot(al, bh))


def turn_groups(x, sign):
    group = lax.broadcasted_iota(jnp.int32, x.shape, 2) // 16
    for d in (4, 2, 1):
        x = jnp.where((group & d) != 0, pltpu.roll(x, d if sign > 0 else 8 - d, 1), x)
    return x


def gather_rows(x):
    return pltpu.roll(turn_groups(x, -1), 0, 2, stride=COLS, stride_axis=1)


def scatter_rows(x):
    row = lax.broadcasted_iota(jnp.int32, x.shape, 1)
    for d in (4, 2, 1):
        x = jnp.where((row & d) != 0, pltpu.roll(x, 128 - COLS * d, 2), x)
    return turn_groups(x, 1)


def aligned(x):
    return pl.multiple_of(x, COLS)


def load_metric(metric, ext, sem, lat):
    start = pl.multiple_of(lat * ROWS, 8)
    low = pl.multiple_of(jnp.maximum(start - 8, 0), 8)
    high = pl.multiple_of(jnp.minimum(start + ROWS, LAT - 8), 8)
    return [
        pltpu.make_async_copy(metric.at[pl.ds(start, ROWS)], ext.at[pl.ds(8, ROWS)], sem.at[0]),
        pltpu.make_async_copy(metric.at[pl.ds(low, 8)], ext.at[pl.ds(0, 8)], sem.at[1]),
        pltpu.make_async_copy(metric.at[pl.ds(high, 8)], ext.at[pl.ds(8 + ROWS, 8)], sem.at[2]),
    ]


def mask_metric(ext, lat):
    ext[0:8, :] = ext[0:8, :] * jnp.where(lat > 0, 1.0, 0.0)
    ext[32:40, :] = ext[32:40, :] * jnp.where(lat < LAT // ROWS - 1, 1.0, 0.0)


def selection(holder):
    hb = jnp.broadcast_to(holder.astype(f32), (MODES, MODES))
    ha = hb.T
    ia = lax.broadcasted_iota(jnp.int32, (MODES, MODES), 0)
    ib = lax.broadcasted_iota(jnp.int32, (MODES, MODES), 1)
    same = jnp.where(ha == hb, 1.0, 0.0)
    before = jnp.where(ia < ib, 1.0, 0.0)
    after = jnp.where(ib < ia, 1.0, 0.0)
    rank_row = jnp.sum(same * before, axis=0, keepdims=True)
    rank_col = jnp.sum(same * after, axis=1, keepdims=True)
    over_row = jnp.where(rank_row >= HOST, 1.0, 0.0)
    over_col = jnp.where(rank_col >= HOST, 1.0, 0.0)
    over_index = jnp.sum(over_col * before, axis=0, keepdims=True)
    patch_a = (ia & (PATCHES - 1)).astype(f32)
    patch_b = (ib & (PATCHES - 1)).astype(f32)
    turn_a = (ia // PATCHES).astype(f32)
    turn_b = (ib // PATCHES).astype(f32)
    count_col = jnp.sum(jnp.where(hb == patch_a, 1.0, 0.0), axis=1, keepdims=True)
    count_row = jnp.sum(jnp.where(ha == patch_b, 1.0, 0.0), axis=0, keepdims=True)
    free_col = jnp.where(turn_a >= count_col, 1.0, 0.0)
    free_row = jnp.where(turn_b >= count_row, 1.0, 0.0)
    free_index = jnp.sum(free_row * after, axis=1, keepdims=True)
    home = jnp.where(ia.astype(f32) == rank_row * PATCHES + hb, 1.0, 0.0)
    guest = free_col * jnp.where(free_index == over_index, 1.0, 0.0)
    hosted = over_row * guest + (1.0 - over_row) * home
    rest = []
    for first in (2, 4):
        rest.append(
            jnp.where(ia.astype(f32) + first * PATCHES == rank_row * PATCHES + hb, 1.0, 0.0)
        )
    return jnp.concatenate([hosted] + rest, axis=0)


def cell_column(row):
    lane = lax.broadcasted_iota(jnp.int32, (COLS, 128), 1)
    sub = lax.broadcasted_iota(jnp.int32, (COLS, 128), 0)
    picked = jnp.where(lane == sub, jnp.broadcast_to(row, (COLS, 128)), 0.0)
    return jnp.broadcast_to(jnp.sum(picked, axis=1, keepdims=True), (COLS, 128))


def patch_kernel(
    u_far, v_far, t_far, q_far, metric, holder, project, depth, sweeps,
    packed, params, hosted, cell_metric, ext,
    u, v, t, q, own, field, edges, chosen, sem, field_sem,
):
    lat = lax.axis_index("lat")
    lon = lax.axis_index("lon")
    metric_copies = load_metric(metric, ext, sem, lat)
    fields = ((u_far, u), (v_far, v), (t_far, t), (q_far, q))
    copies = metric_copies + [
        pltpu.make_async_copy(far, here, field_sem.at[i]) for i, (far, here) in enumerate(fields)
    ]
    for c in copies:
        c.start()
    select = selection(holder[...])
    chosen[...] = select
    hosted[...] = select[: HOST * PATCHES].astype(bf16)
    params[...] = jnp.zeros_like(params)
    count = jnp.sum(jnp.where(holder[...] == lon, 1.0, 0.0), axis=1, keepdims=True)
    for s in range(SLOTS):
        row = chosen[pl.ds(s * PATCHES + lon, 1), :]
        value = jnp.sum(row * depth[...], axis=1, keepdims=True)
        params[0, s : s + 1, :] = jnp.broadcast_to(value, (1, 128))
        value = jnp.sum(row * sweeps[...].astype(f32), axis=1, keepdims=True)
        params[1, s : s + 1, :] = jnp.broadcast_to(value, (1, 128))
        params[2, s : s + 1, :] = jnp.broadcast_to(jnp.where(count > s, 1.0, 0.0), (1, 128))
    sel = select.astype(bf16)
    proj_high, proj_low = split_value(project[...])
    rows_high = jnp.dot(sel, proj_high, preferred_element_type=f32).astype(bf16)
    rows_low = jnp.dot(sel, proj_low, preferred_element_type=f32).astype(bf16)
    for c in metric_copies:
        c.wait()
    mask_metric(ext, lat)

    block = lon // 8
    turn = lon % 8
    offset = turn * COLS

    def lanes(b):
        return ext[:, pl.ds(pl.multiple_of(b * 128, 128), 128)]

    here = lanes(block)
    own[...] = pltpu.roll(here, (128 - offset) % 128, 1)
    west_block = jnp.where(offset == 0, (block + BLOCKS - 1) % BLOCKS, block)
    east_block = jnp.where(offset == 128 - COLS, (block + 1) % BLOCKS, block)
    west_metric = pltpu.roll(lanes(west_block), (129 - offset) % 128, 1)[8:32, 0:1]
    east_metric = pltpu.roll(lanes(east_block), (256 - COLS - offset) % 128, 1)[8:32, 0:1]
    scale = jnp.concatenate([cell_column(own[8 + r : 9 + r, :]) for r in range(ROWS)], axis=0)
    cell_metric[...] = 0.25 * scale
    for c in copies[len(metric_copies) :]:
        c.wait()

    uu = u[...].reshape(CELLS, MODES)
    vv = v[...].reshape(CELLS, MODES)
    virtual = t[...].reshape(CELLS, MODES) * (1.0 + 0.61 * q[...].reshape(CELLS, MODES))
    eighth = 0.125 * virtual
    to_west = eighth - 0.25 * uu
    to_east = eighth + 0.25 * uu
    to_south = eighth - 0.25 * vv
    to_north = eighth + 0.25 * vv
    col = lax.broadcasted_iota(jnp.int32, (CELLS, MODES), 0) & (COLS - 1)
    around = jnp.where(col == COLS - 1, 0.0, pltpu.roll(to_west, CELLS - 1, 0))
    around = around + jnp.where(col == 0, 0.0, pltpu.roll(to_east, 1, 0))
    zero = jnp.zeros((COLS, MODES), f32)
    around = around + jnp.concatenate([to_south[COLS:], zero], axis=0)
    around = around + jnp.concatenate([zero, to_north[: CELLS - COLS]], axis=0)
    forcing = virtual + scale * (around - 0.5 * virtual)
    for r in range(ROWS):
        at = aligned(r // 8 * 128 + COLS * ((turn - r) & 7))
        field[pl.ds(at, COLS), :] = forcing[r * COLS : (r + 1) * COLS]

    edges[...] = jnp.zeros((128, MODES), f32)
    first = t[:, 0, :] * (1.0 + 0.61 * q[:, 0, :])
    last = t[:, COLS - 1, :] * (1.0 + 0.61 * q[:, COLS - 1, :])
    edge_west = jnp.broadcast_to(west_metric, (ROWS, MODES)) * (0.125 * first - 0.25 * u[:, 0, :])
    edge_east = jnp.broadcast_to(east_metric, (ROWS, MODES)) * (
        0.125 * last + 0.25 * u[:, COLS - 1, :]
    )
    for rg in range(3):
        edges[pl.ds(rg, 8, stride=COLS), :] = edge_west[8 * rg : 8 * rg + 8]
        edges[pl.ds(3 + rg, 8, stride=COLS), :] = edge_east[8 * rg : 8 * rg + 8]
    edge_south = cell_column(own[7:8, :]) * to_south[0:COLS]
    edge_north = cell_column(own[32:33, :]) * to_north[CELLS - COLS :]
    edges[8:16, :] = edge_north[0:8]
    edges[24:32, :] = edge_north[8:16]
    edges[104:112, :] = edge_south[0:8]
    edges[120:128, :] = edge_south[8:16]
    order_edges(edges, turn, field, CELLS)

    value = dot3((rows_high, rows_low), split_value(field[...]), ((1,), (1,)))
    for s in range(SLOTS):
        for part in range(4):
            packed[pl.ds(s * 4 + part, PATCHES, stride=4 * SLOTS), :] = value[
                s * PATCHES : (s + 1) * PATCHES, part * 128 : (part + 1) * 128
            ]


def order_edges(source, turn, target, base):
    sub = lax.broadcasted_iota(jnp.int32, (COLS, MODES), 0)
    for g in range(8):
        west = source[pl.ds(aligned(COLS * ((turn - 1 - g) & 7)), COLS), :]
        east = source[pl.ds(aligned(COLS * ((turn + 1 - g) & 7)), COLS), :]
        rim = source[pl.ds(aligned(COLS * ((turn - g) & 7)), COLS), :]
        target[base + COLS * g : base + COLS * g + COLS, :] = jnp.where(
            sub < 3, west, jnp.where(sub < 6, east, rim)
        )


def patch_stage(u, v, t, q, metric, holder, project, depth, sweeps):
    return pl.pallas_call(
        patch_kernel,
        name="patch_stage",

        out_shape=(
            pltpu.VMEM((PATCHES * SLOTS * 4, 128), f32),
            pltpu.VMEM((3, 8, 128), f32),
            pltpu.VMEM((HOST * PATCHES, MODES), bf16),
            pltpu.VMEM((CELLS, MODES), f32),
            pltpu.VMEM((EXT, LON), f32),
        ),
        in_specs=[FAR] * 5 + [VMEM] * 4,
        out_specs=(VMEM,) * 5,
        scratch_shapes=[pltpu.VMEM((ROWS, COLS, MODES), f32)] * 4
        + [
            pltpu.VMEM((EXT, 128), f32),
            pltpu.VMEM((CELLS + 128, MODES), f32),
            pltpu.VMEM((128, MODES), f32),
            pltpu.VMEM((SLOTS * PATCHES, MODES), f32),
            pltpu.SemaphoreType.DMA((3,)),
            pltpu.SemaphoreType.DMA((4,)),
        ],
    )(u, v, t, q, metric, holder, project, depth, sweeps)


def band_kernel(received, band, south, north):
    place = lax.broadcasted_iota(jnp.int32, (PATCHES, 128), 1) & (COLS - 1)
    near_half = (lax.broadcasted_iota(jnp.int32, (BLOCKS, 8, 128), 2) & (COLS - 1)) < 8
    row = lax.broadcasted_iota(jnp.int32, (8, 128), 0)
    for s in range(SLOTS):
        edge = received[pl.ds(s * 4 + 3, PATCHES, stride=4 * SLOTS), :]
        from_east = pltpu.roll(edge, PATCHES - 1, 0)
        from_west = pltpu.roll(edge, 1, 0)
        bands = []
        for rg in range(3):
            x = received[pl.ds(s * 4 + rg, PATCHES, stride=4 * SLOTS), :]
            x = x + jnp.where(place == COLS - 1, pltpu.roll(from_east, 15 - rg, 1), 0.0)
            x = x + jnp.where(place == 0, pltpu.roll(from_west, 128 - 3 - rg, 1), 0.0)
            bands.append(gather_rows(x.reshape(BLOCKS, 8, 128)))
        rim = gather_rows(edge.reshape(BLOCKS, 8, 128))
        low = pltpu.roll(rim, 128 - 8, 2)
        to_north = jnp.where(near_half, low, pltpu.roll(rim, 7, 1))
        to_south = jnp.where(near_half, pltpu.roll(low, 1, 1), rim)
        for b in range(BLOCKS):
            at = slice(b * 128, (b + 1) * 128)
            for rg in range(3):
                band[s, 8 * rg : 8 * rg + 8, at] = bands[rg][b]
            south[s, :, at] = jnp.where(row == 7, to_south[b], bands[0][b])
            north[s, :, at] = jnp.where(row == 0, to_north[b], bands[2][b])


def band_stage(received):
    return pl.pallas_call(
        band_kernel,
        name="band_stage",

        out_shape=(
            pltpu.VMEM((SLOTS, ROWS, LON), f32),
            pltpu.VMEM((SLOTS, 8, LON), f32),
            pltpu.VMEM((SLOTS, 8, LON), f32),
        ),
        in_specs=[VMEM],
        out_specs=(VMEM, VMEM, VMEM),
    )(received)


def solve_slots(
    first, count, band, south, north, from_south, from_north, params, ext, fetches, constants,
    spectral, solved,
):
    cutoff, wave, gain, table_high, table_low, back_high, back_low = constants
    lat = lax.axis_index("lat")
    row = lax.broadcasted_iota(jnp.int32, (8, LON), 0)
    for i in range(count):
        s = first + i
        depth = params[0, s : s + 1, 0:1]
        number = params[1, s : s + 1, 0:1]
        depth = jnp.where(depth > 0.0, depth, 1.0)
        centre = 1.0 + 8.0 * depth
        radius = 8.0 * depth
        relative = centre / radius
        ratio = 1.0 / relative

        def wide(x):
            return jnp.broadcast_to(x, (EXT, LON))

        below = from_south[s]
        above = from_north[s]
        source = jnp.concatenate(
            [
                below + jnp.where(row == 7, south[s], 0.0),
                band[s, 0:8] + jnp.where(row == 0, below, 0.0),
                band[s, 8:16],
                band[s, 16:24] + jnp.where(row == 7, above, 0.0),
                above + jnp.where(row == 0, north[s], 0.0),
            ],
            axis=0,
        )
        coupling = wide(depth) * ext[...]
        direction = source * wide(1.0 / centre)
        residual = source
        total = jnp.zeros_like(source)
        for sweep in range(MAXIT):
            if sweep < MINIT:
                total = total + direction
            else:
                total = total + wide(jnp.where(number > sweep, 1.0, 0.0)) * direction
            if sweep + 1 < MAXIT:
                around = (
                    pltpu.roll(direction, LON - 1, 1)
                    + pltpu.roll(direction, 1, 1)
                    + pltpu.roll(direction, EXT - 1, 0)
                    + pltpu.roll(direction, 1, 0)
                )
                residual = residual - direction + coupling * (around - 4.0 * direction)
                after = 1.0 / (2.0 * relative - ratio)
                direction = (
                    wide(after * ratio) * direction + wide(2.0 * after / radius) * residual
                )
                ratio = after
        x = [total[:, 128 * a : 128 * a + 128] for a in range(BLOCKS)]
        root = math.sqrt(0.5)
        s04, d04 = x[0] + x[4], x[0] - x[4]
        s26, d26 = x[2] + x[6], x[2] - x[6]
        s15, d15 = x[1] + x[5], x[1] - x[5]
        s37, d37 = x[3] + x[7], x[3] - x[7]
        even, odd = s04 + s26, s15 + s37
        lean, turn = root * (d15 - d37), root * (d15 + d37)
        at = slice(i * EXT, (i + 1) * EXT)
        spectral[0, at, 0:128] = even + odd
        spectral[0, at, 128:256] = even - odd
        spectral[1, at, 0:128] = d04 + lean
        spectral[1, at, 128:256] = -d26 - turn
        spectral[2, at, 0:128] = s04 - s26
        spectral[2, at, 128:256] = s37 - s15
        spectral[3, at, 0:128] = d04 - lean
        spectral[3, at, 128:256] = d26 - turn

    for c in fetches:
        c.wait()
    index = lax.broadcasted_iota(jnp.int32, (EXT, 128), 0) + (lat * ROWS - 8)
    lane = lax.broadcasted_iota(jnp.int32, (EXT, 128), 1)
    limit = jnp.zeros((EXT, 1), f32)
    for b in range(LAT // 128):
        picked = jnp.where(
            lane + 128 * b == index, jnp.broadcast_to(cutoff[b : b + 1, :], (EXT, 128)), 0.0
        )
        limit = limit + jnp.sum(picked, axis=1, keepdims=True)
    limit = jnp.where(limit > 0.0, limit, 1.0)
    inverse = 1.0 / (limit * (0.5 * LON))
    for k in range(4):
        table = (table_high[k], table_low[k])
        ratio = jnp.broadcast_to(wave[k : k + 1, :], (EXT, 256)) * jnp.broadcast_to(
            inverse, (EXT, 256)
        )
        ratio = ratio * ratio
        damping = jnp.broadcast_to(gain[k : k + 1, :], (EXT, 256)) / (1.0 + ratio * ratio)
        damping = jnp.concatenate([damping] * count, axis=0)
        spectrum = dot3(split_value(spectral[k, 0 : count * EXT, :]), table, ((1,), (0,)))
        back = (back_high[k], back_low[k])
        spectral[k, 0 : count * EXT, :] = dot3(split_value(spectrum * damping), back, ((1,), (0,)))
    root = math.sqrt(0.5)
    y0 = spectral[0, 0 : count * EXT, 0:128]
    y4 = spectral[0, 0 : count * EXT, 128:256]
    p1, q1 = spectral[1, 0 : count * EXT, 0:128], spectral[1, 0 : count * EXT, 128:256]
    p2, q2 = spectral[2, 0 : count * EXT, 0:128], spectral[2, 0 : count * EXT, 128:256]
    p3, q3 = spectral[3, 0 : count * EXT, 0:128], spectral[3, 0 : count * EXT, 128:256]
    even, odd = y0 + y4, y0 - y4
    a1, b1 = root * p1, root * q1
    a3, b3 = root * p3, root * q3
    swing = q3 - q1
    parts = [None] * 8
    base, side = even + p2, p1 + p3
    parts[0], parts[4] = base + side, base - side
    base, side = even - p2, swing
    parts[2], parts[6] = base + side, base - side
    base, side = odd - q2, (a1 - b1) - (a3 + b3)
    parts[1], parts[5] = base + side, base - side
    base, side = odd + q2, (a3 - b3) - (a1 + b1)
    parts[3], parts[7] = base + side, base - side
    for i in range(count):
        for a in range(BLOCKS):
            solved[i, :, 128 * a : 128 * a + 128] = parts[a][i * EXT : (i + 1) * EXT]


def fetch_all(far, here, sem):
    fetches = [
        pltpu.make_async_copy(source, target, sem.at[i])
        for i, (source, target) in enumerate(zip(far, here))
    ]
    for c in fetches:
        c.start()
    return fetches


def host_kernel(
    band, south, north, from_south, from_north, params, ext,
    *rest,
):
    far_constants, (packed, own_modes, spectral, solved), (*constants, sem) = (
        rest[:7], rest[7:11], rest[11:],
    )
    fetches = fetch_all(far_constants, constants, sem)
    solve_slots(
        0, HOST, band, south, north, from_south, from_north, params, ext, fetches, constants,
        spectral, solved,
    )
    place = lax.broadcasted_iota(jnp.int32, (PATCHES, 128), 1) & (COLS - 1)
    row = lax.broadcasted_iota(jnp.int32, (BLOCKS, 8, 128), 1)
    for i in range(HOST):
        owned = jnp.broadcast_to(params[2, i : i + 1, 0:1], (ROWS, LON))
        own_modes[i] = solved[i, 8:32, :] * owned

        def tile(k):
            return jnp.stack(
                [solved[i, 8 * k : 8 * k + 8, 128 * b : 128 * b + 128] for b in range(BLOCKS)]
            )

        far, close = tile(4), tile(0)
        rim = jnp.where(
            row == 0,
            pltpu.roll(far, 8, 2),
            jnp.where(
                row == 1,
                pltpu.roll(far, 1, 1),
                jnp.where(row == 6, pltpu.roll(pltpu.roll(close, 7, 1), 8, 2), close),
            ),
        )
        edge = scatter_rows(rim).reshape(PATCHES, 128)
        for rg in range(3):
            x = scatter_rows(tile(rg + 1)).reshape(PATCHES, 128)
            packed[pl.ds(i * 4 + rg, PATCHES, stride=4 * HOST), :] = x
            west = pltpu.roll(pltpu.roll(x, 1, 0), 128 - 15 + rg, 1)
            east = pltpu.roll(pltpu.roll(x, PATCHES - 1, 0), 3 + rg, 1)
            edge = jnp.where(place == rg, west, edge)
            edge = jnp.where(place == 3 + rg, east, edge)
        packed[pl.ds(i * 4 + 3, PATCHES, stride=4 * HOST), :] = edge


def solver_scratch(count):
    return [
        pltpu.VMEM((4, count * EXT, 256), f32),
        pltpu.VMEM((count, EXT, LON), f32),
        pltpu.VMEM((LAT // 128, 128), f32),
        pltpu.VMEM((4, 256), f32),
        pltpu.VMEM((4, 256), f32),
        pltpu.VMEM((4, 256, 256), bf16),
        pltpu.VMEM((4, 256, 256), bf16),
        pltpu.VMEM((4, 256, 256), bf16),
        pltpu.VMEM((4, 256, 256), bf16),
        pltpu.SemaphoreType.DMA((7,)),
    ]


def host_stage(*operands):
    return pl.pallas_call(
        host_kernel,
        name="host_stage",

        out_shape=(
            pltpu.VMEM((PATCHES * HOST * 4, 128), f32),
            pltpu.VMEM((HOST, ROWS, LON), f32),
        ),
        in_specs=[VMEM] * 7 + [FAR] * 7,
        out_specs=(VMEM, VMEM),
        scratch_shapes=solver_scratch(HOST),
    )(*operands)


def rest_kernel(
    band, south, north, from_south, from_north, params, ext,
    *rest,
):
    far_constants, rest = rest[:7], rest[7:]
    own_modes, hosted, expand, modes, expand_high, expand_low, spectral, solved = rest[:8]
    *constants, sem = rest[8:]
    fetches = fetch_all(far_constants, constants, sem)
    high, low = split_value(expand[...])
    dims = (((1,), (1,)), ((), ()))
    expand_high[...] = lax.dot_general(
        hosted[...], high, dims, preferred_element_type=f32
    ).astype(bf16)
    expand_low[...] = lax.dot_general(
        hosted[...], low, dims, preferred_element_type=f32
    ).astype(bf16)
    modes[0:HOST] = own_modes[...]
    solve_slots(
        HOST, SLOTS - HOST, band, south, north, from_south, from_north, params, ext, fetches,
        constants, spectral, solved,
    )
    for i in range(SLOTS - HOST):
        modes[HOST + i] = solved[i, 8:32, :]


def rest_stage(*operands):
    return pl.pallas_call(
        rest_kernel,
        name="rest_stage",

        out_shape=(
            jax.ShapeDtypeStruct((SLOTS, ROWS, LON), f32),
            pltpu.VMEM((MODES, MODES), bf16),
            pltpu.VMEM((MODES, MODES), bf16),
        ),
        in_specs=[VMEM] * 7 + [FAR] * 7 + [VMEM] * 3,
        out_specs=(VMEM, VMEM, VMEM),
        scratch_shapes=solver_scratch(SLOTS - HOST),
    )(*operands)


def wind_kernel(
    received, expand_high, expand_low, cell_metric, u_far, v_far, u_new, v_new,
    tall, edges, edge, u, v, sem,
):
    fetches = fetch_all((u_far, v_far), (u, v), sem)
    turn = lax.axis_index("lon") % 8
    table = (expand_high[...], expand_low[...])
    for part in range(4):
        x = jnp.concatenate(
            [received[pl.ds(i * 4 + part, PATCHES, stride=4 * HOST), :] for i in range(HOST)],
            axis=0,
        )
        value = dot3(split_value(x.T), table, ((1,), (0,)))
        if part < 3:
            for g in range(8):
                at = aligned(COLS + part * 128 + COLS * ((turn - g) & 7))
                tall[pl.ds(at, COLS), :] = value[COLS * g : COLS * g + COLS]
        else:
            edges[...] = value
    order_edges(edges, turn, edge, 0)
    tall[0:8, :] = edge[104:112, :]
    tall[8:16, :] = edge[120:128, :]
    tall[CELLS + COLS : CELLS + COLS + 8, :] = edge[8:16, :]
    tall[CELLS + COLS + 8 : CELLS + 2 * COLS, :] = edge[24:32, :]
    pressure = tall[COLS : CELLS + COLS, :]

    def spread(base):
        return jnp.concatenate(
            [
                jnp.broadcast_to(
                    edge[(r % 8) * COLS + base + r // 8 : (r % 8) * COLS + base + r // 8 + 1, :],
                    (COLS, MODES),
                )
                for r in range(ROWS)
            ],
            axis=0,
        )

    col = lax.broadcasted_iota(jnp.int32, (CELLS, MODES), 0) & (COLS - 1)
    east = jnp.where(col == COLS - 1, spread(3), pltpu.roll(pressure, CELLS - 1, 0))
    west = jnp.where(col == 0, spread(0), pltpu.roll(pressure, 1, 0))
    scale = cell_metric[...]
    for c in fetches:
        c.wait()
    u_new[...] = u[...] - (scale * (east - west)).reshape(ROWS, COLS, MODES)
    slope = tall[2 * COLS : CELLS + 2 * COLS, :] - tall[0:CELLS, :]
    v_new[...] = v[...] - (scale * slope).reshape(ROWS, COLS, MODES)


def wind_stage(*operands):
    shape = jax.ShapeDtypeStruct((ROWS, COLS, MODES), f32)
    return pl.pallas_call(
        wind_kernel,
        name="wind_stage",

        out_shape=(shape, shape),
        in_specs=[VMEM] * 4 + [FAR] * 2,
        out_specs=(VMEM, VMEM),
        scratch_shapes=[
            pltpu.VMEM((CELLS + 2 * COLS, MODES), f32),
            pltpu.VMEM((128, MODES), f32),
            pltpu.VMEM((128, MODES), f32),
            pltpu.VMEM((ROWS, COLS, MODES), f32),
            pltpu.VMEM((ROWS, COLS, MODES), f32),
            pltpu.SemaphoreType.DMA((2,)),
        ],
    )(*operands)


def near(*arrays):
    return tuple(pltpu.with_memory_space_constraint(x, pltpu.VMEM) for x in arrays)


def exchange(x, rows):
    x = x.reshape(PATCHES, rows, 128)
    x = lax.all_to_all(x, "lon", split_axis=0, concat_axis=0, tiled=True)
    return x.reshape(PATCHES * rows, 128)


def local(
    eastward_velocity,
    northward_velocity,
    thermal_anomaly,
    water_content,
    gridbox_factor,
    filter_threshold,
    layers_to_eigen,
    eigen_to_layers,
    eigen_screening_factor,
    chebyshev_sweeps,
    eigen_region_holder,
):
    table, wave, gain = filter_tables()
    tables = []
    for x in (table, table.transpose(0, 2, 1)):
        high = np.asarray(x, np.float32).astype(bf16)
        tables += [high, (x - high.astype(np.float64)).astype(np.float32).astype(bf16)]
    constants = [jnp.asarray(x) for x in [wave.astype(np.float32), gain.astype(np.float32)] + tables]
    packed, params, hosted, cell_metric, ext = patch_stage(
        eastward_velocity,
        northward_velocity,
        thermal_anomaly,
        water_content,
        gridbox_factor,
        eigen_region_holder.reshape(1, MODES),
        layers_to_eigen,
        eigen_screening_factor.reshape(1, MODES),
        chebyshev_sweeps.reshape(1, MODES),
    )
    band, south, north = band_stage(*near(exchange(packed, 4 * SLOTS)))
    size = lax.axis_size("lat")
    up = [(i, i + 1) for i in range(size - 1)]
    down = [(j, i) for i, j in up]
    from_south = lax.ppermute(north, "lat", up)
    from_north = lax.ppermute(south, "lat", down)
    solver = near(band, south, north, from_south, from_north, params, ext) + (
        filter_threshold.reshape(LAT // 128, 128), *constants,
    )
    returned, own_modes = host_stage(*solver)
    returned = exchange(returned, 4 * HOST)
    mode_solution, expand_high, expand_low = rest_stage(
        *solver, *near(own_modes, hosted), eigen_to_layers
    )
    u_new, v_new = wind_stage(
        *near(returned, expand_high, expand_low, cell_metric), eastward_velocity, northward_velocity
    )
    return u_new, v_new, mode_solution


def solution(mesh):
    return jax.shard_map(
        local,
        mesh=mesh,
        in_specs=(P("lat", "lon", None),) * 4 + (P(),) * 7,
        out_specs=(P("lat", "lon", None), P("lat", "lon", None), P("lon", "lat", None)),
        check_vma=False,
    )
```

```python
import math

import jax
import jax.numpy as jnp
import numpy as np
from jax import lax
from jax.experimental import pallas as pl
from jax.experimental.pallas import tpu as pltpu
from jax.sharding import PartitionSpec as P

MAXIT = 6
MINIT = 3
ROWS = 24
COLS = 16
CELLS = ROWS * COLS
LON = 1024
LAT = 384
MODES = 128
PATCHES = 64
SLOTS = 6
HOST = 2
REST = 4
EXT = 40
TALL = 32
BLOCKS = LON // 128

f32 = jnp.float32
bf16 = jnp.bfloat16
GRANT = pltpu.CompilerParams(vmem_limit_bytes=24 << 20)
VMEM = pl.BlockSpec(memory_space=pltpu.VMEM)
FAR = pl.BlockSpec(memory_space=pltpu.HBM)


def filter_tables():
    b = np.arange(128)[:, None].astype(np.float64)
    table = np.zeros((4, 256, 256))
    wave = np.zeros((4, 256))
    gain = np.zeros((4, 256))
    k2 = np.arange(65)[None, :]
    angle = 2 * np.pi * b * k2 / 128
    table[0, :128, :65] = np.cos(angle)
    table[0, :128, 65:128] = np.sin(angle[:, 1:64])
    wave[0, :65] = 8 * np.arange(65)
    wave[0, 65:128] = 8 * np.arange(1, 64)
    gain[0, :128] = 2.0
    gain[0, 0] = gain[0, 64] = 1.0
    k2 = np.arange(64)[None, :]
    angle = 2 * np.pi * b * (4 + 8 * k2) / 1024
    table[0, 128:, 128:192] = np.cos(angle)
    table[0, 128:, 192:] = np.sin(angle)
    wave[0, 128:192] = wave[0, 192:] = 4 + 8 * np.arange(64)
    gain[0, 128:] = 2.0
    for k1 in (1, 2, 3):
        k = k1 + 8 * np.arange(128)
        angle = 2 * np.pi * b * k[None, :] / 1024
        c, s = np.cos(angle), np.sin(angle)
        table[k1, :128, :128] = c
        table[k1, :128, 128:] = -s
        table[k1, 128:, :128] = s
        table[k1, 128:, 128:] = c
        wave[k1, :128] = wave[k1, 128:] = np.minimum(k, 1024 - k)
        gain[k1] = 2.0
    return table, wave, gain / LON


def split_value(x):
    high = x.astype(bf16)
    low = (x - high.astype(f32)).astype(bf16)
    return high, low


def dot3(a, b, dims):
    ah, al = a
    bh, bl = b

    def dot(x, y):
        return lax.dot_general(x, y, (dims, ((), ())), preferred_element_type=f32)

    return dot(ah, bh) + (dot(ah, bl) + dot(al, bh))


def turn_groups(x, sign):
    group = lax.broadcasted_iota(jnp.int32, x.shape, 2) // 16
    for d in (4, 2, 1):
        x = jnp.where((group & d) != 0, pltpu.roll(x, d if sign > 0 else 8 - d, 1), x)
    return x


def gather_rows(x):
    return pltpu.roll(turn_groups(x, -1), 0, 2, stride=COLS, stride_axis=1)


def scatter_rows(x):
    row = lax.broadcasted_iota(jnp.int32, x.shape, 1)
    for d in (4, 2, 1):
        x = jnp.where((row & d) != 0, pltpu.roll(x, 128 - COLS * d, 2), x)
    return turn_groups(x, 1)


def aligned(x):
    return pl.multiple_of(x, COLS)


def load_metric(metric, ext, sem, lat):
    start = pl.multiple_of(lat * ROWS, 8)
    low = pl.multiple_of(jnp.maximum(start - 8, 0), 8)
    high = pl.multiple_of(jnp.minimum(start + ROWS, LAT - 8), 8)
    return [
        pltpu.make_async_copy(metric.at[pl.ds(start, ROWS)], ext.at[pl.ds(8, ROWS)], sem.at[0]),
        pltpu.make_async_copy(metric.at[pl.ds(low, 8)], ext.at[pl.ds(0, 8)], sem.at[1]),
        pltpu.make_async_copy(metric.at[pl.ds(high, 8)], ext.at[pl.ds(8 + ROWS, 8)], sem.at[2]),
    ]


def mask_metric(ext, lat):
    ext[0:8, :] = ext[0:8, :] * jnp.where(lat > 0, 1.0, 0.0)
    ext[32:40, :] = ext[32:40, :] * jnp.where(lat < LAT // ROWS - 1, 1.0, 0.0)


def selection(holder):
    hb = jnp.broadcast_to(holder.astype(f32), (MODES, MODES))
    ha = hb.T
    ia = lax.broadcasted_iota(jnp.int32, (MODES, MODES), 0)
    ib = lax.broadcasted_iota(jnp.int32, (MODES, MODES), 1)
    same = jnp.where(ha == hb, 1.0, 0.0)
    before = jnp.where(ia < ib, 1.0, 0.0)
    after = jnp.where(ib < ia, 1.0, 0.0)
    rank_row = jnp.sum(same * before, axis=0, keepdims=True)
    rank_col = jnp.sum(same * after, axis=1, keepdims=True)
    over_row = jnp.where(rank_row >= HOST, 1.0, 0.0)
    over_col = jnp.where(rank_col >= HOST, 1.0, 0.0)
    over_index = jnp.sum(over_col * before, axis=0, keepdims=True)
    patch_a = (ia & (PATCHES - 1)).astype(f32)
    patch_b = (ib & (PATCHES - 1)).astype(f32)
    turn_a = (ia // PATCHES).astype(f32)
    turn_b = (ib // PATCHES).astype(f32)
    count_col = jnp.sum(jnp.where(hb == patch_a, 1.0, 0.0), axis=1, keepdims=True)
    count_row = jnp.sum(jnp.where(ha == patch_b, 1.0, 0.0), axis=0, keepdims=True)
    free_col = jnp.where(turn_a >= count_col, 1.0, 0.0)
    free_row = jnp.where(turn_b >= count_row, 1.0, 0.0)
    free_index = jnp.sum(free_row * after, axis=1, keepdims=True)
    home = jnp.where(ia.astype(f32) == rank_row * PATCHES + hb, 1.0, 0.0)
    guest = free_col * jnp.where(free_index == over_index, 1.0, 0.0)
    hosted = over_row * guest + (1.0 - over_row) * home
    rest = []
    for first in (2, 4):
        rest.append(
            jnp.where(ia.astype(f32) + first * PATCHES == rank_row * PATCHES + hb, 1.0, 0.0)
        )
    return jnp.concatenate([hosted] + rest, axis=0)


def cell_column(row):
    lane = lax.broadcasted_iota(jnp.int32, (COLS, 128), 1)
    sub = lax.broadcasted_iota(jnp.int32, (COLS, 128), 0)
    picked = jnp.where(lane == sub, jnp.broadcast_to(row, (COLS, 128)), 0.0)
    return jnp.broadcast_to(jnp.sum(picked, axis=1, keepdims=True), (COLS, 128))


def patch_kernel(
    u_far, v_far, t_far, q_far, metric, holder, project, depth, sweeps,
    packed, params, hosted, cell_metric, ext,
    u, v, t, q, own, field, edges, chosen, sem, field_sem,
):
    lat = lax.axis_index("lat")
    lon = lax.axis_index("lon")
    metric_copies = load_metric(metric, ext, sem, lat)
    fields = ((u_far, u), (v_far, v), (t_far, t), (q_far, q))
    copies = metric_copies + [
        pltpu.make_async_copy(far, here, field_sem.at[i]) for i, (far, here) in enumerate(fields)
    ]
    for c in copies:
        c.start()
    select = selection(holder[...])
    chosen[...] = select
    hosted[...] = select[: HOST * PATCHES].astype(bf16)
    params[...] = jnp.zeros_like(params)
    count = jnp.sum(jnp.where(holder[...] == lon, 1.0, 0.0), axis=1, keepdims=True)
    for s in range(SLOTS):
        row = chosen[pl.ds(s * PATCHES + lon, 1), :]
        value = jnp.sum(row * depth[...], axis=1, keepdims=True)
        params[0, s : s + 1, :] = jnp.broadcast_to(value, (1, 128))
        value = jnp.sum(row * sweeps[...].astype(f32), axis=1, keepdims=True)
        params[1, s : s + 1, :] = jnp.broadcast_to(value, (1, 128))
        params[2, s : s + 1, :] = jnp.broadcast_to(jnp.where(count > s, 1.0, 0.0), (1, 128))
    sel = select.astype(bf16)
    proj_high, proj_low = split_value(project[...])
    rows_high = jnp.dot(sel, proj_high, preferred_element_type=f32).astype(bf16)
    rows_low = jnp.dot(sel, proj_low, preferred_element_type=f32).astype(bf16)
    for c in metric_copies:
        c.wait()
    mask_metric(ext, lat)

    block = lon // 8
    turn = lon % 8
    offset = turn * COLS

    def lanes(b):
        return ext[:, pl.ds(pl.multiple_of(b * 128, 128), 128)]

    here = lanes(block)
    own[...] = pltpu.roll(here, (128 - offset) % 128, 1)
    west_block = jnp.where(offset == 0, (block + BLOCKS - 1) % BLOCKS, block)
    east_block = jnp.where(offset == 128 - COLS, (block + 1) % BLOCKS, block)
    west_metric = pltpu.roll(lanes(west_block), (129 - offset) % 128, 1)[8:32, 0:1]
    east_metric = pltpu.roll(lanes(east_block), (256 - COLS - offset) % 128, 1)[8:32, 0:1]
    scale = jnp.concatenate([cell_column(own[8 + r : 9 + r, :]) for r in range(ROWS)], axis=0)
    cell_metric[...] = 0.25 * scale
    for c in copies[len(metric_copies) :]:
        c.wait()

    uu = u[...].reshape(CELLS, MODES)
    vv = v[...].reshape(CELLS, MODES)
    virtual = t[...].reshape(CELLS, MODES) * (1.0 + 0.61 * q[...].reshape(CELLS, MODES))
    eighth = 0.125 * virtual
    to_west = eighth - 0.25 * uu
    to_east = eighth + 0.25 * uu
    to_south = eighth - 0.25 * vv
    to_north = eighth + 0.25 * vv
    col = lax.broadcasted_iota(jnp.int32, (CELLS, MODES), 0) & (COLS - 1)
    around = jnp.where(col == COLS - 1, 0.0, pltpu.roll(to_west, CELLS - 1, 0))
    around = around + jnp.where(col == 0, 0.0, pltpu.roll(to_east, 1, 0))
    zero = jnp.zeros((COLS, MODES), f32)
    around = around + jnp.concatenate([to_south[COLS:], zero], axis=0)
    around = around + jnp.concatenate([zero, to_north[: CELLS - COLS]], axis=0)
    forcing = virtual + scale * (around - 0.5 * virtual)
    for r in range(ROWS):
        at = aligned(r // 8 * 128 + COLS * ((turn - r) & 7))
        field[pl.ds(at, COLS), :] = forcing[r * COLS : (r + 1) * COLS]

    edges[...] = jnp.zeros((128, MODES), f32)
    first = t[:, 0, :] * (1.0 + 0.61 * q[:, 0, :])
    last = t[:, COLS - 1, :] * (1.0 + 0.61 * q[:, COLS - 1, :])
    edge_west = jnp.broadcast_to(west_metric, (ROWS, MODES)) * (0.125 * first - 0.25 * u[:, 0, :])
    edge_east = jnp.broadcast_to(east_metric, (ROWS, MODES)) * (
        0.125 * last + 0.25 * u[:, COLS - 1, :]
    )
    for rg in range(3):
        edges[pl.ds(rg, 8, stride=COLS), :] = edge_west[8 * rg : 8 * rg + 8]
        edges[pl.ds(3 + rg, 8, stride=COLS), :] = edge_east[8 * rg : 8 * rg + 8]
    edge_south = cell_column(own[7:8, :]) * to_south[0:COLS]
    edge_north = cell_column(own[32:33, :]) * to_north[CELLS - COLS :]
    edges[8:16, :] = edge_north[0:8]
    edges[24:32, :] = edge_north[8:16]
    edges[104:112, :] = edge_south[0:8]
    edges[120:128, :] = edge_south[8:16]
    order_edges(edges, turn, field, CELLS)

    value = dot3((rows_high, rows_low), split_value(field[...]), ((1,), (1,)))
    for s in range(SLOTS):
        for part in range(4):
            packed[pl.ds(s * 4 + part, PATCHES, stride=4 * SLOTS), :] = value[
                s * PATCHES : (s + 1) * PATCHES, part * 128 : (part + 1) * 128
            ]


def order_edges(source, turn, target, base):
    sub = lax.broadcasted_iota(jnp.int32, (COLS, MODES), 0)
    for g in range(8):
        west = source[pl.ds(aligned(COLS * ((turn - 1 - g) & 7)), COLS), :]
        east = source[pl.ds(aligned(COLS * ((turn + 1 - g) & 7)), COLS), :]
        rim = source[pl.ds(aligned(COLS * ((turn - g) & 7)), COLS), :]
        target[base + COLS * g : base + COLS * g + COLS, :] = jnp.where(
            sub < 3, west, jnp.where(sub < 6, east, rim)
        )


def patch_stage(u, v, t, q, metric, holder, project, depth, sweeps):
    return pl.pallas_call(
        patch_kernel,
        name="patch_stage",

        out_shape=(
            pltpu.VMEM((PATCHES * SLOTS * 4, 128), f32),
            pltpu.VMEM((3, 8, 128), f32),
            pltpu.VMEM((HOST * PATCHES, MODES), bf16),
            pltpu.VMEM((CELLS, MODES), f32),
            pltpu.VMEM((EXT, LON), f32),
        ),
        in_specs=[FAR] * 5 + [VMEM] * 4,
        out_specs=(VMEM,) * 5,
        scratch_shapes=[pltpu.VMEM((ROWS, COLS, MODES), f32)] * 4
        + [
            pltpu.VMEM((EXT, 128), f32),
            pltpu.VMEM((CELLS + 128, MODES), f32),
            pltpu.VMEM((128, MODES), f32),
            pltpu.VMEM((SLOTS * PATCHES, MODES), f32),
            pltpu.SemaphoreType.DMA((3,)),
            pltpu.SemaphoreType.DMA((4,)),
        ],
    )(u, v, t, q, metric, holder, project, depth, sweeps)


def spread_rows(row, block, count=8):
    return pl.ds(row * BLOCKS + block, count, stride=BLOCKS)


def band_kernel(received, band, south, north):
    place = lax.broadcasted_iota(jnp.int32, (PATCHES, 128), 1) & (COLS - 1)
    near_half = (lax.broadcasted_iota(jnp.int32, (BLOCKS, 8, 128), 2) & (COLS - 1)) < 8
    row = lax.broadcasted_iota(jnp.int32, (8, 128), 0)
    for s in range(SLOTS):
        edge = received[pl.ds(s * 4 + 3, PATCHES, stride=4 * SLOTS), :]
        from_east = pltpu.roll(edge, PATCHES - 1, 0)
        from_west = pltpu.roll(edge, 1, 0)
        bands = []
        for rg in range(3):
            x = received[pl.ds(s * 4 + rg, PATCHES, stride=4 * SLOTS), :]
            x = x + jnp.where(place == COLS - 1, pltpu.roll(from_east, 15 - rg, 1), 0.0)
            x = x + jnp.where(place == 0, pltpu.roll(from_west, 128 - 3 - rg, 1), 0.0)
            bands.append(gather_rows(x.reshape(BLOCKS, 8, 128)))
        rim = gather_rows(edge.reshape(BLOCKS, 8, 128))
        low = pltpu.roll(rim, 128 - 8, 2)
        to_north = jnp.where(near_half, low, pltpu.roll(rim, 7, 1))
        to_south = jnp.where(near_half, pltpu.roll(low, 1, 1), rim)
        for b in range(BLOCKS):
            for rg in range(3):
                band[spread_rows(s * ROWS + 8 * rg, b), :] = bands[rg][b]
            south[spread_rows(s * 8, b), :] = jnp.where(row == 7, to_south[b], bands[0][b])
            north[spread_rows(s * 8, b), :] = jnp.where(row == 0, to_north[b], bands[2][b])


def band_stage(received):
    return pl.pallas_call(
        band_kernel,
        name="band_stage",

        out_shape=(
            pltpu.VMEM((SLOTS * ROWS * BLOCKS, 128), f32),
            pltpu.VMEM((SLOTS * 8 * BLOCKS, 128), f32),
            pltpu.VMEM((SLOTS * 8 * BLOCKS, 128), f32),
        ),
        in_specs=[VMEM],
        out_specs=(VMEM, VMEM, VMEM),
    )(received)


def solve_slots(
    first, count, edge, band, south, north, from_south, from_north, params, metric, damping,
    fetches, constants, totals, spectral, solved,
):
    table_high, table_low, back_high, back_low = constants
    height = solved.shape[1]
    reach = MAXIT - 1 + edge
    out = ROWS + 2 * edge

    def neighbours(x):
        lane = lax.broadcasted_iota(jnp.int32, x.shape, 2)
        east = pltpu.roll(x, 127, 2)
        east = jnp.where(lane == 127, pltpu.roll(east, BLOCKS - 1, 1), east)
        west = pltpu.roll(x, 1, 2)
        west = jnp.where(lane == 0, pltpu.roll(west, 1, 1), west)
        return east + west

    for i in range(count):
        s = first + i
        depth = params[0, s : s + 1, 0:1]
        number = params[1, s : s + 1, 0:1]
        depth = jnp.where(depth > 0.0, depth, 1.0)
        centre = 1.0 + 8.0 * depth
        radius = 8.0 * depth
        relative = centre / radius
        ratio = 1.0 / relative

        def wide(x):
            return jnp.broadcast_to(x, (BLOCKS, 128))[None]


        def rows_of(source, rows):
            x = source[s * rows * BLOCKS : (s + 1) * rows * BLOCKS, :]
            return x.reshape(rows, BLOCKS, 128)

        below, above, mine = rows_of(from_south, 8), rows_of(from_north, 8), rows_of(band, ROWS)
        residual = jnp.concatenate(
            [
                below[8 - reach : 7],
                below[7:8] + rows_of(south, 8)[7:8],
                mine[0:1] + below[0:1],
                mine[1:23],
                mine[23:24] + above[7:8],
                above[0:1] + rows_of(north, 8)[0:1],
                above[1:reach],
            ],
            axis=0,
        )
        height_now = ROWS + 2 * reach - 2
        at = (8 - reach + 1) * BLOCKS
        coupling = wide(depth) * metric[at : at + height_now * BLOCKS, :].reshape(
            height_now, BLOCKS, 128
        )
        direction = residual * wide(1.0 / centre)
        total = direction[MAXIT - 1 : MAXIT - 1 + out]
        for sweep in range(1, MAXIT):
            middle = direction[1:-1]
            around = neighbours(middle) + (direction[2:] + direction[:-2])
            residual = residual[1:-1] - middle + coupling * (around - 4.0 * middle)
            coupling = coupling[1:-1]
            after = 1.0 / (2.0 * relative - ratio)
            direction = wide(after * ratio) * middle + wide(2.0 * after / radius) * residual
            ratio = after
            low = MAXIT - 1 - sweep
            if sweep < MINIT:
                total = total + direction[low : low + out]
            else:
                active = wide(jnp.where(number > sweep, 1.0, 0.0))
                total = total + active * direction[low : low + out]
        at = i * height * BLOCKS
        if edge:
            parts = [total[1 : ROWS + 2], total[0:1]]
            parts.append(jnp.zeros((height - ROWS - 2, BLOCKS, 128), f32))
            total = jnp.concatenate(parts, axis=0)
        totals[at : at + height * BLOCKS, :] = total.reshape(height * BLOCKS, 128)
        x = [totals[spread_rows(i * height, a, height), :] for a in range(BLOCKS)]
        root = math.sqrt(0.5)
        s04, d04 = x[0] + x[4], x[0] - x[4]
        s26, d26 = x[2] + x[6], x[2] - x[6]
        s15, d15 = x[1] + x[5], x[1] - x[5]
        s37, d37 = x[3] + x[7], x[3] - x[7]
        even, odd = s04 + s26, s15 + s37
        lean, turn = root * (d15 - d37), root * (d15 + d37)
        at = slice(i * height, (i + 1) * height)
        spectral[0, at, 0:128] = even + odd
        spectral[0, at, 128:256] = even - odd
        spectral[1, at, 0:128] = d04 + lean
        spectral[1, at, 128:256] = -d26 - turn
        spectral[2, at, 0:128] = s04 - s26
        spectral[2, at, 128:256] = s37 - s15
        spectral[3, at, 0:128] = d04 - lean
        spectral[3, at, 128:256] = d26 - turn

    for c in fetches:
        c.wait()
    for k in range(4):
        table = (table_high[k], table_low[k])
        weight = jnp.concatenate([damping[k, 0:height, :]] * count, axis=0)
        spectrum = dot3(split_value(spectral[k, 0 : count * height, :]), table, ((1,), (0,)))
        back = (back_high[k], back_low[k])
        spectral[k, 0 : count * height, :] = dot3(split_value(spectrum * weight), back, ((1,), (0,)))
    root = math.sqrt(0.5)
    y0 = spectral[0, 0 : count * height, 0:128]
    y4 = spectral[0, 0 : count * height, 128:256]
    p1, q1 = spectral[1, 0 : count * height, 0:128], spectral[1, 0 : count * height, 128:256]
    p2, q2 = spectral[2, 0 : count * height, 0:128], spectral[2, 0 : count * height, 128:256]
    p3, q3 = spectral[3, 0 : count * height, 0:128], spectral[3, 0 : count * height, 128:256]
    even, odd = y0 + y4, y0 - y4
    a1, b1 = root * p1, root * q1
    a3, b3 = root * p3, root * q3
    swing = q3 - q1
    parts = [None] * 8
    base, side = even + p2, p1 + p3
    parts[0], parts[4] = base + side, base - side
    base, side = even - p2, swing
    parts[2], parts[6] = base + side, base - side
    base, side = odd - q2, (a1 - b1) - (a3 + b3)
    parts[1], parts[5] = base + side, base - side
    base, side = odd + q2, (a3 - b3) - (a1 + b1)
    parts[3], parts[7] = base + side, base - side
    for i in range(count):
        for a in range(BLOCKS):
            solved[i, :, 128 * a : 128 * a + 128] = parts[a][i * height : (i + 1) * height]


def damping_kernel(ext, cutoff, wave, gain, damping, metric):
    for tile in range(EXT // 8):
        for b in range(BLOCKS):
            metric[spread_rows(8 * tile, b), :] = ext[
                8 * tile : 8 * tile + 8, 128 * b : 128 * b + 128
            ]
    start = lax.axis_index("lat") * ROWS
    sub = lax.broadcasted_iota(jnp.int32, (TALL, 128), 0)
    index = jnp.where(sub == ROWS + 1, start - 1, start + sub)
    lane = lax.broadcasted_iota(jnp.int32, (TALL, 128), 1)
    limit = jnp.zeros((TALL, 1), f32)
    for b in range(LAT // 128):
        picked = jnp.where(
            lane + 128 * b == index, jnp.broadcast_to(cutoff[b : b + 1, :], (TALL, 128)), 0.0
        )
        limit = limit + jnp.sum(picked, axis=1, keepdims=True)
    limit = jnp.where(limit > 0.0, limit, 1.0)
    inverse = jnp.broadcast_to(1.0 / (limit * (0.5 * LON)), (TALL, 256))
    for k in range(4):
        ratio = jnp.broadcast_to(wave[k : k + 1, :], (TALL, 256)) * inverse
        ratio = ratio * ratio
        damping[k] = jnp.broadcast_to(gain[k : k + 1, :], (TALL, 256)) / (1.0 + ratio * ratio)


def damping_stage(*operands):
    return pl.pallas_call(
        damping_kernel,
        name="damping_stage",
        out_shape=(
            pltpu.VMEM((4, TALL, 256), f32),
            pltpu.VMEM((EXT * BLOCKS, 128), f32),
        ),
        in_specs=[VMEM] * 4,
        out_specs=(VMEM, VMEM),
    )(*operands)


def fetch_all(far, here, sem):
    fetches = [
        pltpu.make_async_copy(source, target, sem.at[i])
        for i, (source, target) in enumerate(zip(far, here))
    ]
    for c in fetches:
        c.start()
    return fetches


def host_kernel(
    band, south, north, from_south, from_north, params, metric, damping,
    *rest,
):
    far_constants, (packed, own_modes, totals, spectral, solved), (*constants, sem) = (
        rest[:4], rest[4:9], rest[9:],
    )
    fetches = fetch_all(far_constants, constants, sem)
    solve_slots(
        0, HOST, 1, band, south, north, from_south, from_north, params, metric, damping, fetches,
        constants, totals, spectral, solved,
    )
    place = lax.broadcasted_iota(jnp.int32, (PATCHES, 128), 1) & (COLS - 1)
    row = lax.broadcasted_iota(jnp.int32, (BLOCKS, 8, 128), 1)
    for i in range(HOST):
        owned = jnp.broadcast_to(params[2, i : i + 1, 0:1], (ROWS, LON))
        own_modes[i] = solved[i, 0:ROWS, :] * owned

        def tile(k):
            return jnp.stack(
                [solved[i, 8 * k : 8 * k + 8, 128 * b : 128 * b + 128] for b in range(BLOCKS)]
            )

        last = tile(3)
        shifted = pltpu.roll(last, 8, 2)
        rim = jnp.where(
            row == 0,
            shifted,
            jnp.where(
                row == 1,
                pltpu.roll(last, 1, 1),
                jnp.where(row == 6, pltpu.roll(shifted, 5, 1), pltpu.roll(last, 6, 1)),
            ),
        )
        edge = scatter_rows(rim).reshape(PATCHES, 128)
        for rg in range(3):
            x = scatter_rows(tile(rg)).reshape(PATCHES, 128)
            packed[pl.ds(i * 4 + rg, PATCHES, stride=4 * HOST), :] = x
            west = pltpu.roll(pltpu.roll(x, 1, 0), 128 - 15 + rg, 1)
            east = pltpu.roll(pltpu.roll(x, PATCHES - 1, 0), 3 + rg, 1)
            edge = jnp.where(place == rg, west, edge)
            edge = jnp.where(place == 3 + rg, east, edge)
        packed[pl.ds(i * 4 + 3, PATCHES, stride=4 * HOST), :] = edge


def solver_scratch(count, height):
    return [
        pltpu.VMEM((count * height * BLOCKS, 128), f32),
        pltpu.VMEM((4, count * height, 256), f32),
        pltpu.VMEM((count, height, LON), f32),
        pltpu.VMEM((4, 256, 256), bf16),
        pltpu.VMEM((4, 256, 256), bf16),
        pltpu.VMEM((4, 256, 256), bf16),
        pltpu.VMEM((4, 256, 256), bf16),
        pltpu.SemaphoreType.DMA((4,)),
    ]


def host_stage(*operands):
    return pl.pallas_call(
        host_kernel,
        name="host_stage",

        out_shape=(
            pltpu.VMEM((PATCHES * HOST * 4, 128), f32),
            pltpu.VMEM((HOST, ROWS, LON), f32),
        ),
        in_specs=[VMEM] * 8 + [FAR] * 4,
        out_specs=(VMEM, VMEM),
        scratch_shapes=solver_scratch(HOST, TALL),
    )(*operands)


def rest_kernel(
    band, south, north, from_south, from_north, params, metric, damping,
    *rest,
):
    far_constants, rest = rest[:4], rest[4:]
    own_modes, hosted, expand, modes, expand_high, expand_low = rest[:6]
    totals, spectral, solved, *constants, sem = rest[6:]
    fetches = fetch_all(far_constants, constants, sem)
    high, low = split_value(expand[...])
    dims = (((1,), (1,)), ((), ()))
    expand_high[...] = lax.dot_general(
        hosted[...], high, dims, preferred_element_type=f32
    ).astype(bf16)
    expand_low[...] = lax.dot_general(
        hosted[...], low, dims, preferred_element_type=f32
    ).astype(bf16)
    modes[0:HOST] = own_modes[...]
    solve_slots(
        HOST, REST, 0, band, south, north, from_south, from_north, params, metric, damping, fetches,
        constants, totals, spectral, solved,
    )
    for i in range(REST):
        modes[HOST + i] = solved[i]


def rest_stage(*operands):
    return pl.pallas_call(
        rest_kernel,
        name="rest_stage",

        out_shape=(
            jax.ShapeDtypeStruct((SLOTS, ROWS, LON), f32),
            pltpu.VMEM((MODES, MODES), bf16),
            pltpu.VMEM((MODES, MODES), bf16),
        ),
        in_specs=[VMEM] * 8 + [FAR] * 4 + [VMEM] * 3,
        out_specs=(VMEM, VMEM, VMEM),
        scratch_shapes=solver_scratch(REST, ROWS),
    )(*operands)


def wind_kernel(
    received, expand_high, expand_low, cell_metric, u_far, v_far, u_new, v_new,
    tall, edges, edge, u, v, sem,
):
    fetches = fetch_all((u_far, v_far), (u, v), sem)
    turn = lax.axis_index("lon") % 8
    table = (expand_high[...], expand_low[...])
    for part in range(4):
        x = jnp.concatenate(
            [received[pl.ds(i * 4 + part, PATCHES, stride=4 * HOST), :] for i in range(HOST)],
            axis=0,
        )
        value = dot3(split_value(x.T), table, ((1,), (0,)))
        if part < 3:
            for g in range(8):
                at = aligned(COLS + part * 128 + COLS * ((turn - g) & 7))
                tall[pl.ds(at, COLS), :] = value[COLS * g : COLS * g + COLS]
        else:
            edges[...] = value
    order_edges(edges, turn, edge, 0)
    tall[0:8, :] = edge[104:112, :]
    tall[8:16, :] = edge[120:128, :]
    tall[CELLS + COLS : CELLS + COLS + 8, :] = edge[8:16, :]
    tall[CELLS + COLS + 8 : CELLS + 2 * COLS, :] = edge[24:32, :]
    pressure = tall[COLS : CELLS + COLS, :]

    def spread(base):
        return jnp.concatenate(
            [
                jnp.broadcast_to(
                    edge[(r % 8) * COLS + base + r // 8 : (r % 8) * COLS + base + r // 8 + 1, :],
                    (COLS, MODES),
                )
                for r in range(ROWS)
            ],
            axis=0,
        )

    col = lax.broadcasted_iota(jnp.int32, (CELLS, MODES), 0) & (COLS - 1)
    east = jnp.where(col == COLS - 1, spread(3), pltpu.roll(pressure, CELLS - 1, 0))
    west = jnp.where(col == 0, spread(0), pltpu.roll(pressure, 1, 0))
    scale = cell_metric[...]
    for c in fetches:
        c.wait()
    u_new[...] = u[...] - (scale * (east - west)).reshape(ROWS, COLS, MODES)
    slope = tall[2 * COLS : CELLS + 2 * COLS, :] - tall[0:CELLS, :]
    v_new[...] = v[...] - (scale * slope).reshape(ROWS, COLS, MODES)


def wind_stage(*operands):
    shape = jax.ShapeDtypeStruct((ROWS, COLS, MODES), f32)
    return pl.pallas_call(
        wind_kernel,
        name="wind_stage",

        out_shape=(shape, shape),
        in_specs=[VMEM] * 4 + [FAR] * 2,
        out_specs=(VMEM, VMEM),
        scratch_shapes=[
            pltpu.VMEM((CELLS + 2 * COLS, MODES), f32),
            pltpu.VMEM((128, MODES), f32),
            pltpu.VMEM((128, MODES), f32),
            pltpu.VMEM((ROWS, COLS, MODES), f32),
            pltpu.VMEM((ROWS, COLS, MODES), f32),
            pltpu.SemaphoreType.DMA((2,)),
        ],
    )(*operands)


def near(*arrays):
    return tuple(pltpu.with_memory_space_constraint(x, pltpu.VMEM) for x in arrays)


def exchange(x, rows):
    x = x.reshape(PATCHES, rows, 128)
    x = lax.all_to_all(x, "lon", split_axis=0, concat_axis=0, tiled=True)
    return x.reshape(PATCHES * rows, 128)


def local(
    eastward_velocity,
    northward_velocity,
    thermal_anomaly,
    water_content,
    gridbox_factor,
    filter_threshold,
    layers_to_eigen,
    eigen_to_layers,
    eigen_screening_factor,
    chebyshev_sweeps,
    eigen_region_holder,
):
    table, wave, gain = filter_tables()
    tables = []
    for x in (table, table.transpose(0, 2, 1)):
        high = np.asarray(x, np.float32).astype(bf16)
        tables += [high, (x - high.astype(np.float64)).astype(np.float32).astype(bf16)]
    constants = [jnp.asarray(x) for x in [wave.astype(np.float32), gain.astype(np.float32)] + tables]
    packed, params, hosted, cell_metric, ext = patch_stage(
        eastward_velocity,
        northward_velocity,
        thermal_anomaly,
        water_content,
        gridbox_factor,
        eigen_region_holder.reshape(1, MODES),
        layers_to_eigen,
        eigen_screening_factor.reshape(1, MODES),
        chebyshev_sweeps.reshape(1, MODES),
    )
    wave, gain, *constants = constants

    band, south, north = band_stage(*near(exchange(packed, 4 * SLOTS)))
    size = lax.axis_size("lat")
    up = [(i, i + 1) for i in range(size - 1)]
    down = [(j, i) for i, j in up]
    from_south = lax.ppermute(north, "lat", up)
    from_north = lax.ppermute(south, "lat", down)
    damping, metric = damping_stage(
        *near(ext), filter_threshold.reshape(LAT // 128, 128), wave, gain
    )
    solver = near(band, south, north, from_south, from_north, params, metric, damping) + tuple(
        constants
    )
    returned, own_modes = host_stage(*solver)
    returned = exchange(returned, 4 * HOST)
    mode_solution, expand_high, expand_low = rest_stage(
        *solver, *near(own_modes, hosted), eigen_to_layers
    )
    u_new, v_new = wind_stage(
        *near(returned, expand_high, expand_low, cell_metric), eastward_velocity, northward_velocity
    )
    return u_new, v_new, mode_solution


def solution(mesh):
    return jax.shard_map(
        local,
        mesh=mesh,
        in_specs=(P("lat", "lon", None),) * 4 + (P(),) * 7,
        out_specs=(P("lat", "lon", None), P("lat", "lon", None), P("lon", "lat", None)),
        check_vma=False,
    )
```

```python
import math

import jax
import jax.numpy as jnp
import numpy as np
from jax import lax
from jax.experimental import pallas as pl
from jax.experimental.pallas import tpu as pltpu
from jax.sharding import PartitionSpec as P

MAXIT = 6
MINIT = 3
ROWS = 24
COLS = 16
CELLS = ROWS * COLS
LON = 1024
LAT = 384
MODES = 128
PATCHES = 64
SLOTS = 6
HOST = 2
REST = 4
EXT = 40
TALL = 32
BLOCKS = LON // 128

f32 = jnp.float32
bf16 = jnp.bfloat16
GRANT = pltpu.CompilerParams(vmem_limit_bytes=24 << 20)
VMEM = pl.BlockSpec(memory_space=pltpu.VMEM)
FAR = pl.BlockSpec(memory_space=pltpu.HBM)


def filter_tables():
    b = np.arange(128)[:, None].astype(np.float64)
    table = np.zeros((4, 256, 256))
    wave = np.zeros((4, 256))
    gain = np.zeros((4, 256))
    k2 = np.arange(65)[None, :]
    angle = 2 * np.pi * b * k2 / 128
    table[0, :128, :65] = np.cos(angle)
    table[0, :128, 65:128] = np.sin(angle[:, 1:64])
    wave[0, :65] = 8 * np.arange(65)
    wave[0, 65:128] = 8 * np.arange(1, 64)
    gain[0, :128] = 2.0
    gain[0, 0] = gain[0, 64] = 1.0
    k2 = np.arange(64)[None, :]
    angle = 2 * np.pi * b * (4 + 8 * k2) / 1024
    table[0, 128:, 128:192] = np.cos(angle)
    table[0, 128:, 192:] = np.sin(angle)
    wave[0, 128:192] = wave[0, 192:] = 4 + 8 * np.arange(64)
    gain[0, 128:] = 2.0
    for k1 in (1, 2, 3):
        k = k1 + 8 * np.arange(128)
        angle = 2 * np.pi * b * k[None, :] / 1024
        c, s = np.cos(angle), np.sin(angle)
        table[k1, :128, :128] = c
        table[k1, :128, 128:] = -s
        table[k1, 128:, :128] = s
        table[k1, 128:, 128:] = c
        wave[k1, :128] = wave[k1, 128:] = np.minimum(k, 1024 - k)
        gain[k1] = 2.0
    return table, wave, gain / LON


def split_value(x):
    high = x.astype(bf16)
    low = (x - high.astype(f32)).astype(bf16)
    return high, low


def dot3(a, b, dims):
    ah, al = a
    bh, bl = b

    def dot(x, y):
        return lax.dot_general(x, y, (dims, ((), ())), preferred_element_type=f32)

    return dot(ah, bh) + (dot(ah, bl) + dot(al, bh))


def turn_groups(x, sign):
    group = lax.broadcasted_iota(jnp.int32, x.shape, 2) // 16
    for d in (4, 2, 1):
        x = jnp.where((group & d) != 0, pltpu.roll(x, d if sign > 0 else 8 - d, 1), x)
    return x


def gather_rows(x):
    return pltpu.roll(turn_groups(x, -1), 0, 2, stride=COLS, stride_axis=1)


def scatter_rows(x):
    row = lax.broadcasted_iota(jnp.int32, x.shape, 1)
    for d in (4, 2, 1):
        x = jnp.where((row & d) != 0, pltpu.roll(x, 128 - COLS * d, 2), x)
    return turn_groups(x, 1)


def aligned(x):
    return pl.multiple_of(x, COLS)


def load_metric(metric, ext, sem, lat):
    start = pl.multiple_of(lat * ROWS, 8)
    low = pl.multiple_of(jnp.maximum(start - 8, 0), 8)
    high = pl.multiple_of(jnp.minimum(start + ROWS, LAT - 8), 8)
    return [
        pltpu.make_async_copy(metric.at[pl.ds(start, ROWS)], ext.at[pl.ds(8, ROWS)], sem.at[0]),
        pltpu.make_async_copy(metric.at[pl.ds(low, 8)], ext.at[pl.ds(0, 8)], sem.at[1]),
        pltpu.make_async_copy(metric.at[pl.ds(high, 8)], ext.at[pl.ds(8 + ROWS, 8)], sem.at[2]),
    ]


def mask_metric(ext, lat):
    ext[0:8, :] = ext[0:8, :] * jnp.where(lat > 0, 1.0, 0.0)
    ext[32:40, :] = ext[32:40, :] * jnp.where(lat < LAT // ROWS - 1, 1.0, 0.0)


def selection(holder):
    hb = jnp.broadcast_to(holder.astype(f32), (MODES, MODES))
    ha = hb.T
    ia = lax.broadcasted_iota(jnp.int32, (MODES, MODES), 0)
    ib = lax.broadcasted_iota(jnp.int32, (MODES, MODES), 1)
    same = jnp.where(ha == hb, 1.0, 0.0)
    before = jnp.where(ia < ib, 1.0, 0.0)
    after = jnp.where(ib < ia, 1.0, 0.0)
    rank_row = jnp.sum(same * before, axis=0, keepdims=True)
    rank_col = jnp.sum(same * after, axis=1, keepdims=True)
    over_row = jnp.where(rank_row >= HOST, 1.0, 0.0)
    over_col = jnp.where(rank_col >= HOST, 1.0, 0.0)
    over_index = jnp.sum(over_col * before, axis=0, keepdims=True)
    patch_a = (ia & (PATCHES - 1)).astype(f32)
    patch_b = (ib & (PATCHES - 1)).astype(f32)
    turn_a = (ia // PATCHES).astype(f32)
    turn_b = (ib // PATCHES).astype(f32)
    count_col = jnp.sum(jnp.where(hb == patch_a, 1.0, 0.0), axis=1, keepdims=True)
    count_row = jnp.sum(jnp.where(ha == patch_b, 1.0, 0.0), axis=0, keepdims=True)
    free_col = jnp.where(turn_a >= count_col, 1.0, 0.0)
    free_row = jnp.where(turn_b >= count_row, 1.0, 0.0)
    free_index = jnp.sum(free_row * after, axis=1, keepdims=True)
    home = jnp.where(ia.astype(f32) == rank_row * PATCHES + hb, 1.0, 0.0)
    guest = free_col * jnp.where(free_index == over_index, 1.0, 0.0)
    hosted = over_row * guest + (1.0 - over_row) * home
    rest = []
    for first in (2, 4):
        rest.append(
            jnp.where(ia.astype(f32) + first * PATCHES == rank_row * PATCHES + hb, 1.0, 0.0)
        )
    return jnp.concatenate([hosted] + rest, axis=0)


def cell_column(row):
    lane = lax.broadcasted_iota(jnp.int32, (COLS, 128), 1)
    sub = lax.broadcasted_iota(jnp.int32, (COLS, 128), 0)
    picked = jnp.where(lane == sub, jnp.broadcast_to(row, (COLS, 128)), 0.0)
    return jnp.broadcast_to(jnp.sum(picked, axis=1, keepdims=True), (COLS, 128))


def patch_kernel(
    u_far, v_far, t_far, q_far, metric, holder, project, depth, sweeps,
    packed, params, hosted, ext,
    u, v, t, q, own, field, edges, chosen, sem, field_sem,
):
    lat = lax.axis_index("lat")
    lon = lax.axis_index("lon")
    metric_copies = load_metric(metric, ext, sem, lat)
    fields = ((u_far, u), (v_far, v), (t_far, t), (q_far, q))
    copies = metric_copies + [
        pltpu.make_async_copy(far, here, field_sem.at[i]) for i, (far, here) in enumerate(fields)
    ]
    for c in copies:
        c.start()
    select = selection(holder[...])
    chosen[...] = select
    hosted[...] = select[: HOST * PATCHES].astype(bf16)
    params[...] = jnp.zeros_like(params)
    count = jnp.sum(jnp.where(holder[...] == lon, 1.0, 0.0), axis=1, keepdims=True)
    for s in range(SLOTS):
        row = chosen[pl.ds(s * PATCHES + lon, 1), :]
        value = jnp.sum(row * depth[...], axis=1, keepdims=True)
        params[0, s : s + 1, :] = jnp.broadcast_to(value, (1, 128))
        value = jnp.sum(row * sweeps[...].astype(f32), axis=1, keepdims=True)
        params[1, s : s + 1, :] = jnp.broadcast_to(value, (1, 128))
        params[2, s : s + 1, :] = jnp.broadcast_to(jnp.where(count > s, 1.0, 0.0), (1, 128))
    sel = select.astype(bf16)
    proj_high, proj_low = split_value(project[...])
    rows_high = jnp.dot(sel, proj_high, preferred_element_type=f32).astype(bf16)
    rows_low = jnp.dot(sel, proj_low, preferred_element_type=f32).astype(bf16)
    for c in metric_copies:
        c.wait()
    mask_metric(ext, lat)

    block = lon // 8
    turn = lon % 8
    offset = turn * COLS

    def lanes(b):
        return ext[:, pl.ds(pl.multiple_of(b * 128, 128), 128)]

    here = lanes(block)
    own[...] = pltpu.roll(here, (128 - offset) % 128, 1)
    west_block = jnp.where(offset == 0, (block + BLOCKS - 1) % BLOCKS, block)
    east_block = jnp.where(offset == 128 - COLS, (block + 1) % BLOCKS, block)
    west_metric = pltpu.roll(lanes(west_block), (129 - offset) % 128, 1)[8:32, 0:1]
    east_metric = pltpu.roll(lanes(east_block), (256 - COLS - offset) % 128, 1)[8:32, 0:1]
    scale = jnp.concatenate([cell_column(own[8 + r : 9 + r, :]) for r in range(ROWS)], axis=0)
    for c in copies[len(metric_copies) :]:
        c.wait()

    uu = u[...].reshape(CELLS, MODES)
    vv = v[...].reshape(CELLS, MODES)
    virtual = t[...].reshape(CELLS, MODES) * (1.0 + 0.61 * q[...].reshape(CELLS, MODES))
    eighth = 0.125 * virtual
    to_west = eighth - 0.25 * uu
    to_east = eighth + 0.25 * uu
    to_south = eighth - 0.25 * vv
    to_north = eighth + 0.25 * vv
    col = lax.broadcasted_iota(jnp.int32, (CELLS, MODES), 0) & (COLS - 1)
    around = jnp.where(col == COLS - 1, 0.0, pltpu.roll(to_west, CELLS - 1, 0))
    around = around + jnp.where(col == 0, 0.0, pltpu.roll(to_east, 1, 0))
    zero = jnp.zeros((COLS, MODES), f32)
    around = around + jnp.concatenate([to_south[COLS:], zero], axis=0)
    around = around + jnp.concatenate([zero, to_north[: CELLS - COLS]], axis=0)
    forcing = virtual + scale * (around - 0.5 * virtual)
    for r in range(ROWS):
        at = aligned(r // 8 * 128 + COLS * ((turn - r) & 7))
        field[pl.ds(at, COLS), :] = forcing[r * COLS : (r + 1) * COLS]

    edges[...] = jnp.zeros((128, MODES), f32)
    first = t[:, 0, :] * (1.0 + 0.61 * q[:, 0, :])
    last = t[:, COLS - 1, :] * (1.0 + 0.61 * q[:, COLS - 1, :])
    edge_west = jnp.broadcast_to(west_metric, (ROWS, MODES)) * (0.125 * first - 0.25 * u[:, 0, :])
    edge_east = jnp.broadcast_to(east_metric, (ROWS, MODES)) * (
        0.125 * last + 0.25 * u[:, COLS - 1, :]
    )
    for rg in range(3):
        edges[pl.ds(rg, 8, stride=COLS), :] = edge_west[8 * rg : 8 * rg + 8]
        edges[pl.ds(3 + rg, 8, stride=COLS), :] = edge_east[8 * rg : 8 * rg + 8]
    edge_south = cell_column(own[7:8, :]) * to_south[0:COLS]
    edge_north = cell_column(own[32:33, :]) * to_north[CELLS - COLS :]
    edges[8:16, :] = edge_north[0:8]
    edges[24:32, :] = edge_north[8:16]
    edges[104:112, :] = edge_south[0:8]
    edges[120:128, :] = edge_south[8:16]
    order_edges(edges, turn, field, CELLS)

    value = dot3((rows_high, rows_low), split_value(field[...]), ((1,), (1,)))
    for s in range(SLOTS):
        for part in range(4):
            packed[pl.ds(s * 4 + part, PATCHES, stride=4 * SLOTS), :] = value[
                s * PATCHES : (s + 1) * PATCHES, part * 128 : (part + 1) * 128
            ]


def order_edges(source, turn, target, base):
    sub = lax.broadcasted_iota(jnp.int32, (COLS, MODES), 0)
    for g in range(8):
        west = source[pl.ds(aligned(COLS * ((turn - 1 - g) & 7)), COLS), :]
        east = source[pl.ds(aligned(COLS * ((turn + 1 - g) & 7)), COLS), :]
        rim = source[pl.ds(aligned(COLS * ((turn - g) & 7)), COLS), :]
        target[base + COLS * g : base + COLS * g + COLS, :] = jnp.where(
            sub < 3, west, jnp.where(sub < 6, east, rim)
        )


def patch_stage(u, v, t, q, metric, holder, project, depth, sweeps):
    return pl.pallas_call(
        patch_kernel,
        name="patch_stage",

        out_shape=(
            pltpu.VMEM((PATCHES * SLOTS * 4, 128), f32),
            pltpu.VMEM((3, 8, 128), f32),
            pltpu.VMEM((HOST * PATCHES, MODES), bf16),
            pltpu.VMEM((EXT, LON), f32),
        ),
        in_specs=[FAR] * 5 + [VMEM] * 4,
        out_specs=(VMEM,) * 4,
        scratch_shapes=[pltpu.VMEM((ROWS, COLS, MODES), f32)] * 4
        + [
            pltpu.VMEM((EXT, 128), f32),
            pltpu.VMEM((CELLS + 128, MODES), f32),
            pltpu.VMEM((128, MODES), f32),
            pltpu.VMEM((SLOTS * PATCHES, MODES), f32),
            pltpu.SemaphoreType.DMA((3,)),
            pltpu.SemaphoreType.DMA((4,)),
        ],
    )(u, v, t, q, metric, holder, project, depth, sweeps)


def spread_rows(row, block, count=8):
    return pl.ds(row * BLOCKS + block, count, stride=BLOCKS)


def band_kernel(received, band, south, north):
    place = lax.broadcasted_iota(jnp.int32, (PATCHES, 128), 1) & (COLS - 1)
    near_half = (lax.broadcasted_iota(jnp.int32, (BLOCKS, 8, 128), 2) & (COLS - 1)) < 8
    row = lax.broadcasted_iota(jnp.int32, (8, 128), 0)
    for s in range(SLOTS):
        edge = received[pl.ds(s * 4 + 3, PATCHES, stride=4 * SLOTS), :]
        from_east = pltpu.roll(edge, PATCHES - 1, 0)
        from_west = pltpu.roll(edge, 1, 0)
        bands = []
        for rg in range(3):
            x = received[pl.ds(s * 4 + rg, PATCHES, stride=4 * SLOTS), :]
            x = x + jnp.where(place == COLS - 1, pltpu.roll(from_east, 15 - rg, 1), 0.0)
            x = x + jnp.where(place == 0, pltpu.roll(from_west, 128 - 3 - rg, 1), 0.0)
            bands.append(gather_rows(x.reshape(BLOCKS, 8, 128)))
        rim = gather_rows(edge.reshape(BLOCKS, 8, 128))
        low = pltpu.roll(rim, 128 - 8, 2)
        to_north = jnp.where(near_half, low, pltpu.roll(rim, 7, 1))
        to_south = jnp.where(near_half, pltpu.roll(low, 1, 1), rim)
        for b in range(BLOCKS):
            for rg in range(3):
                band[spread_rows(s * ROWS + 8 * rg, b), :] = bands[rg][b]
            south[spread_rows(s * 8, b), :] = jnp.where(row == 7, to_south[b], bands[0][b])
            north[spread_rows(s * 8, b), :] = jnp.where(row == 0, to_north[b], bands[2][b])


def band_stage(received):
    return pl.pallas_call(
        band_kernel,
        name="band_stage",

        out_shape=(
            pltpu.VMEM((SLOTS * ROWS * BLOCKS, 128), f32),
            pltpu.VMEM((SLOTS * 8 * BLOCKS, 128), f32),
            pltpu.VMEM((SLOTS * 8 * BLOCKS, 128), f32),
        ),
        in_specs=[VMEM],
        out_specs=(VMEM, VMEM, VMEM),
    )(received)


def split_eight(x, spectral, row):
    root = math.sqrt(0.5)
    s04, d04 = x[0] + x[4], x[0] - x[4]
    s26, d26 = x[2] + x[6], x[2] - x[6]
    s15, d15 = x[1] + x[5], x[1] - x[5]
    s37, d37 = x[3] + x[7], x[3] - x[7]
    even, odd = s04 + s26, s15 + s37
    lean, turn = root * (d15 - d37), root * (d15 + d37)
    at = slice(row, row + 8)
    spectral[0, at, 0:128] = even + odd
    spectral[0, at, 128:256] = even - odd
    spectral[1, at, 0:128] = d04 + lean
    spectral[1, at, 128:256] = -d26 - turn
    spectral[2, at, 0:128] = s04 - s26
    spectral[2, at, 128:256] = s37 - s15
    spectral[3, at, 0:128] = d04 - lean
    spectral[3, at, 128:256] = d26 - turn


def join_eight(spectral, row):
    root = math.sqrt(0.5)
    at = slice(row, row + 8)
    y0, y4 = spectral[0, at, 0:128], spectral[0, at, 128:256]
    p1, q1 = spectral[1, at, 0:128], spectral[1, at, 128:256]
    p2, q2 = spectral[2, at, 0:128], spectral[2, at, 128:256]
    p3, q3 = spectral[3, at, 0:128], spectral[3, at, 128:256]
    even, odd = y0 + y4, y0 - y4
    lean = root * ((p1 - p3) - (q1 + q3))
    turn = root * ((p3 - p1) - (q1 + q3))
    side, swing = p1 + p3, q3 - q1
    up, down = even + p2, even - p2
    left, right = odd - q2, odd + q2
    return (
        up + side, left + lean, down + swing, right + turn,
        up - side, left - lean, down - swing, right - turn,
    )


def solve_slots(
    first, count, edge, band, south, north, from_south, from_north, params, metric, damping,
    fetches, constants, totals, spectral, solved,
):
    table_high, table_low, back_high, back_low = constants
    height = solved.shape[1]
    reach = MAXIT - 1 + edge
    out = ROWS + 2 * edge

    def rows_list(x):
        return [x[r : r + 1] for r in range(x.shape[0])]

    def neighbours(x):
        lane = lax.broadcasted_iota(jnp.int32, x.shape, 2)
        east = pltpu.roll(x, 127, 2)
        east = jnp.where(lane == 127, pltpu.roll(east, BLOCKS - 1, 1), east)
        west = pltpu.roll(x, 1, 2)
        west = jnp.where(lane == 0, pltpu.roll(west, 1, 1), west)
        return east + west

    for i in range(count):
        s = first + i
        depth = params[0, s : s + 1, 0:1]
        number = params[1, s : s + 1, 0:1]
        depth = jnp.where(depth > 0.0, depth, 1.0)
        centre = 1.0 + 8.0 * depth
        radius = 8.0 * depth
        relative = centre / radius
        ratio = 1.0 / relative

        def wide(x):
            return jnp.broadcast_to(x, (BLOCKS, 128))[None]


        def rows_of(source, rows):
            x = source[s * rows * BLOCKS : (s + 1) * rows * BLOCKS, :]
            return x.reshape(rows, BLOCKS, 128)

        below, above, mine = rows_of(from_south, 8), rows_of(from_north, 8), rows_of(band, ROWS)
        residual = jnp.concatenate(
            [
                below[8 - reach : 7],
                below[7:8] + rows_of(south, 8)[7:8],
                mine[0:1] + below[0:1],
                mine[1:23],
                mine[23:24] + above[7:8],
                above[0:1] + rows_of(north, 8)[0:1],
                above[1:reach],
            ],
            axis=0,
        )
        height_now = ROWS + 2 * reach - 2
        at = (8 - reach + 1) * BLOCKS
        coupling = wide(depth) * metric[at : at + height_now * BLOCKS, :].reshape(
            height_now, BLOCKS, 128
        )
        direction = residual * wide(1.0 / centre)
        total = rows_list(direction[MAXIT - 1 : MAXIT - 1 + out])
        direction, residual, coupling = map(rows_list, (direction, residual, coupling))
        for sweep in range(1, MAXIT):
            after = 1.0 / (2.0 * relative - ratio)
            keep, push = wide(after * ratio), wide(2.0 * after / radius)
            active = wide(jnp.where(number > sweep, 1.0, 0.0))
            ratio = after
            low = MAXIT - 1 - sweep
            fresh, left = [], []
            for r in range(len(direction) - 2):
                middle = direction[r + 1]
                around = neighbours(middle) + (direction[r] + direction[r + 2])
                rest = residual[r + 1] - middle + coupling[r + sweep - 1] * (around - 4.0 * middle)
                left.append(rest)
                fresh.append(keep * middle + push * rest)
                if low <= r < low + out:
                    gain = fresh[r] if sweep < MINIT else active * fresh[r]
                    total[r - low] = total[r - low] + gain
            direction, residual = fresh, left
        total = jnp.concatenate(total, axis=0)
        at = i * height * BLOCKS
        if edge:
            parts = [total[1 : ROWS + 2], total[0:1]]
            parts.append(jnp.zeros((height - ROWS - 2, BLOCKS, 128), f32))
            total = jnp.concatenate(parts, axis=0)
        totals[at : at + height * BLOCKS, :] = total.reshape(height * BLOCKS, 128)
        for row in range(i * height, (i + 1) * height, 8):
            split_eight([totals[spread_rows(row, a), :] for a in range(BLOCKS)], spectral, row)
    for c in fetches:
        c.wait()
    for k in range(4):
        table = (table_high[k], table_low[k])
        weight = jnp.concatenate([damping[k, 0:height, :]] * count, axis=0)
        spectrum = dot3(split_value(spectral[k, 0 : count * height, :]), table, ((1,), (0,)))
        back = (back_high[k], back_low[k])
        spectral[k, 0 : count * height, :] = dot3(split_value(spectrum * weight), back, ((1,), (0,)))
    for row in range(0, count * height, 8):
        i, start = row // height, row % height
        for a, part in enumerate(join_eight(spectral, row)):
            solved[i, start : start + 8, 128 * a : 128 * a + 128] = part


def damping_kernel(ext, cutoff, wave, gain, damping, metric):
    for tile in range(EXT // 8):
        for b in range(BLOCKS):
            metric[spread_rows(8 * tile, b), :] = ext[
                8 * tile : 8 * tile + 8, 128 * b : 128 * b + 128
            ]
    start = lax.axis_index("lat") * ROWS
    sub = lax.broadcasted_iota(jnp.int32, (TALL, 128), 0)
    index = jnp.where(sub == ROWS + 1, start - 1, start + sub)
    lane = lax.broadcasted_iota(jnp.int32, (TALL, 128), 1)
    limit = jnp.zeros((TALL, 1), f32)
    for b in range(LAT // 128):
        picked = jnp.where(
            lane + 128 * b == index, jnp.broadcast_to(cutoff[b : b + 1, :], (TALL, 128)), 0.0
        )
        limit = limit + jnp.sum(picked, axis=1, keepdims=True)
    limit = jnp.where(limit > 0.0, limit, 1.0)
    inverse = jnp.broadcast_to(1.0 / (limit * (0.5 * LON)), (TALL, 256))
    for k in range(4):
        ratio = jnp.broadcast_to(wave[k : k + 1, :], (TALL, 256)) * inverse
        ratio = ratio * ratio
        damping[k] = jnp.broadcast_to(gain[k : k + 1, :], (TALL, 256)) / (1.0 + ratio * ratio)


def damping_stage(*operands):
    return pl.pallas_call(
        damping_kernel,
        name="damping_stage",
        out_shape=(
            pltpu.VMEM((4, TALL, 256), f32),
            pltpu.VMEM((EXT * BLOCKS, 128), f32),
        ),
        in_specs=[VMEM] * 4,
        out_specs=(VMEM, VMEM),
    )(*operands)


def fetch_all(far, here, sem):
    fetches = [
        pltpu.make_async_copy(source, target, sem.at[i])
        for i, (source, target) in enumerate(zip(far, here))
    ]
    for c in fetches:
        c.start()
    return fetches


def host_kernel(
    band, south, north, from_south, from_north, params, metric, damping,
    *rest,
):
    far_constants, (packed, own_modes, totals, spectral, solved), (*constants, sem) = (
        rest[:4], rest[4:9], rest[9:],
    )
    fetches = fetch_all(far_constants, constants, sem)
    solve_slots(
        0, HOST, 1, band, south, north, from_south, from_north, params, metric, damping, fetches,
        constants, totals, spectral, solved,
    )
    place = lax.broadcasted_iota(jnp.int32, (PATCHES, 128), 1) & (COLS - 1)
    row = lax.broadcasted_iota(jnp.int32, (BLOCKS, 8, 128), 1)
    for i in range(HOST):
        owned = jnp.broadcast_to(params[2, i : i + 1, 0:1], (ROWS, LON))
        own_modes[i] = solved[i, 0:ROWS, :] * owned

        def tile(k):
            return jnp.stack(
                [solved[i, 8 * k : 8 * k + 8, 128 * b : 128 * b + 128] for b in range(BLOCKS)]
            )

        last = tile(3)
        shifted = pltpu.roll(last, 8, 2)
        rim = jnp.where(
            row == 0,
            shifted,
            jnp.where(
                row == 1,
                pltpu.roll(last, 1, 1),
                jnp.where(row == 6, pltpu.roll(shifted, 5, 1), pltpu.roll(last, 6, 1)),
            ),
        )
        edge = scatter_rows(rim).reshape(PATCHES, 128)
        for rg in range(3):
            x = scatter_rows(tile(rg)).reshape(PATCHES, 128)
            packed[pl.ds(i * 4 + rg, PATCHES, stride=4 * HOST), :] = x
            west = pltpu.roll(pltpu.roll(x, 1, 0), 128 - 15 + rg, 1)
            east = pltpu.roll(pltpu.roll(x, PATCHES - 1, 0), 3 + rg, 1)
            edge = jnp.where(place == rg, west, edge)
            edge = jnp.where(place == 3 + rg, east, edge)
        packed[pl.ds(i * 4 + 3, PATCHES, stride=4 * HOST), :] = edge


def solver_scratch(count, height):
    return [
        pltpu.VMEM((count * height * BLOCKS, 128), f32),
        pltpu.VMEM((4, count * height, 256), f32),
        pltpu.VMEM((count, height, LON), f32),
        pltpu.VMEM((4, 256, 256), bf16),
        pltpu.VMEM((4, 256, 256), bf16),
        pltpu.VMEM((4, 256, 256), bf16),
        pltpu.VMEM((4, 256, 256), bf16),
        pltpu.SemaphoreType.DMA((4,)),
    ]


def host_stage(*operands):
    return pl.pallas_call(
        host_kernel,
        name="host_stage",

        out_shape=(
            pltpu.VMEM((PATCHES * HOST * 4, 128), f32),
            pltpu.VMEM((HOST, ROWS, LON), f32),
        ),
        in_specs=[VMEM] * 8 + [FAR] * 4,
        out_specs=(VMEM, VMEM),
        scratch_shapes=solver_scratch(HOST, TALL),
    )(*operands)


def rest_kernel(
    band, south, north, from_south, from_north, params, metric, damping,
    *rest,
):
    far_constants, rest = rest[:4], rest[4:]
    own_modes, hosted, expand, u_far, v_far, modes, expand_high, expand_low, u, v = rest[:10]
    cell_metric, totals, spectral, solved, *constants, sem, wind_sem, own = rest[10:]
    winds = fetch_all((u_far, v_far), (u, v), wind_sem)
    fetches = fetch_all(far_constants, constants, sem)
    high, low = split_value(expand[...])
    dims = (((1,), (1,)), ((), ()))
    expand_high[...] = lax.dot_general(
        hosted[...], high, dims, preferred_element_type=f32
    ).astype(bf16)
    expand_low[...] = lax.dot_general(
        hosted[...], low, dims, preferred_element_type=f32
    ).astype(bf16)
    modes[0:HOST] = own_modes[...]
    solve_slots(
        HOST, REST, 0, band, south, north, from_south, from_north, params, metric, damping, fetches,
        constants, totals, spectral, solved,
    )
    for i in range(REST):
        modes[HOST + i] = solved[i]
    lon = lax.axis_index("lon")
    own[...] = pltpu.roll(
        metric[spread_rows(8, lon // 8, ROWS), :], (128 - lon % 8 * COLS) % 128, 1
    )
    for r in range(ROWS):
        cell_metric[r * COLS : (r + 1) * COLS, :] = 0.25 * cell_column(own[r : r + 1, :])
    for c in winds:
        c.wait()


def rest_stage(*operands):
    return pl.pallas_call(
        rest_kernel,
        name="rest_stage",

        out_shape=(
            jax.ShapeDtypeStruct((SLOTS, ROWS, LON), f32),
            pltpu.VMEM((MODES, MODES), bf16),
            pltpu.VMEM((MODES, MODES), bf16),
            pltpu.VMEM((ROWS, COLS, MODES), f32),
            pltpu.VMEM((ROWS, COLS, MODES), f32),
            pltpu.VMEM((CELLS, MODES), f32),
        ),
        in_specs=[VMEM] * 8 + [FAR] * 4 + [VMEM] * 3 + [FAR] * 2,
        out_specs=(VMEM,) * 6,
        scratch_shapes=solver_scratch(REST, ROWS)
        + [pltpu.SemaphoreType.DMA((2,)), pltpu.VMEM((ROWS, 128), f32)],
    )(*operands)


def wind_kernel(
    received, expand_high, expand_low, cell_metric, u, v, u_new, v_new, tall, edges, edge
):
    turn = lax.axis_index("lon") % 8
    table = (expand_high[...], expand_low[...])
    for part in range(4):
        x = jnp.concatenate(
            [received[pl.ds(i * 4 + part, PATCHES, stride=4 * HOST), :] for i in range(HOST)],
            axis=0,
        )
        value = dot3(split_value(x.T), table, ((1,), (0,)))
        if part < 3:
            for g in range(8):
                at = aligned(COLS + part * 128 + COLS * ((turn - g) & 7))
                tall[pl.ds(at, COLS), :] = value[COLS * g : COLS * g + COLS]
        else:
            edges[...] = value
    order_edges(edges, turn, edge, 0)
    tall[0:8, :] = edge[104:112, :]
    tall[8:16, :] = edge[120:128, :]
    tall[CELLS + COLS : CELLS + COLS + 8, :] = edge[8:16, :]
    tall[CELLS + COLS + 8 : CELLS + 2 * COLS, :] = edge[24:32, :]
    pressure = tall[COLS : CELLS + COLS, :]

    def spread(base):
        return jnp.concatenate(
            [
                jnp.broadcast_to(
                    edge[(r % 8) * COLS + base + r // 8 : (r % 8) * COLS + base + r // 8 + 1, :],
                    (COLS, MODES),
                )
                for r in range(ROWS)
            ],
            axis=0,
        )

    col = lax.broadcasted_iota(jnp.int32, (CELLS, MODES), 0) & (COLS - 1)
    east = jnp.where(col == COLS - 1, spread(3), pltpu.roll(pressure, CELLS - 1, 0))
    west = jnp.where(col == 0, spread(0), pltpu.roll(pressure, 1, 0))
    scale = cell_metric[...]
    u_new[...] = u[...] - (scale * (east - west)).reshape(ROWS, COLS, MODES)
    slope = tall[2 * COLS : CELLS + 2 * COLS, :] - tall[0:CELLS, :]
    v_new[...] = v[...] - (scale * slope).reshape(ROWS, COLS, MODES)


def wind_stage(*operands):
    shape = jax.ShapeDtypeStruct((ROWS, COLS, MODES), f32)
    return pl.pallas_call(
        wind_kernel,
        name="wind_stage",

        out_shape=(shape, shape),
        in_specs=[VMEM] * 6,
        out_specs=(VMEM, VMEM),
        scratch_shapes=[
            pltpu.VMEM((CELLS + 2 * COLS, MODES), f32),
            pltpu.VMEM((128, MODES), f32),
            pltpu.VMEM((128, MODES), f32),
        ],
    )(*operands)


def near(*arrays):
    return tuple(pltpu.with_memory_space_constraint(x, pltpu.VMEM) for x in arrays)


def exchange(x, rows):
    x = x.reshape(PATCHES, rows, 128)
    x = lax.all_to_all(x, "lon", split_axis=0, concat_axis=0, tiled=True)
    return x.reshape(PATCHES * rows, 128)


def local(
    eastward_velocity,
    northward_velocity,
    thermal_anomaly,
    water_content,
    gridbox_factor,
    filter_threshold,
    layers_to_eigen,
    eigen_to_layers,
    eigen_screening_factor,
    chebyshev_sweeps,
    eigen_region_holder,
):
    table, wave, gain = filter_tables()
    tables = []
    for x in (table, table.transpose(0, 2, 1)):
        high = np.asarray(x, np.float32).astype(bf16)
        tables += [high, (x - high.astype(np.float64)).astype(np.float32).astype(bf16)]
    constants = [jnp.asarray(x) for x in [wave.astype(np.float32), gain.astype(np.float32)] + tables]
    packed, params, hosted, ext = patch_stage(
        eastward_velocity,
        northward_velocity,
        thermal_anomaly,
        water_content,
        gridbox_factor,
        eigen_region_holder.reshape(1, MODES),
        layers_to_eigen,
        eigen_screening_factor.reshape(1, MODES),
        chebyshev_sweeps.reshape(1, MODES),
    )
    wave, gain, *constants = constants

    band, south, north = band_stage(*near(exchange(packed, 4 * SLOTS)))
    size = lax.axis_size("lat")
    up = [(i, i + 1) for i in range(size - 1)]
    down = [(j, i) for i, j in up]
    from_south = lax.ppermute(north, "lat", up)
    from_north = lax.ppermute(south, "lat", down)
    damping, metric = damping_stage(
        *near(ext), filter_threshold.reshape(LAT // 128, 128), wave, gain
    )
    solver = near(band, south, north, from_south, from_north, params, metric, damping) + tuple(
        constants
    )
    returned, own_modes = host_stage(*solver)
    returned = exchange(returned, 4 * HOST)
    mode_solution, expand_high, expand_low, u, v, cell_metric = rest_stage(
        *solver, *near(own_modes, hosted), eigen_to_layers, eastward_velocity, northward_velocity
    )
    u_new, v_new = wind_stage(
        *near(returned, expand_high, expand_low, cell_metric, u, v)
    )
    return u_new, v_new, mode_solution


def solution(mesh):
    return jax.shard_map(
        local,
        mesh=mesh,
        in_specs=(P("lat", "lon", None),) * 4 + (P(),) * 7,
        out_specs=(P("lat", "lon", None), P("lat", "lon", None), P("lon", "lat", None)),
        check_vma=False,
    )
```

```python
import math

import jax
import jax.numpy as jnp
import numpy as np
from jax import lax
from jax.experimental import pallas as pl
from jax.experimental.pallas import tpu as pltpu
from jax.sharding import PartitionSpec as P

MAXIT = 6
MINIT = 3
ROWS = 24
COLS = 16
CELLS = ROWS * COLS
LON = 1024
LAT = 384
MODES = 128
PATCHES = 64
SLOTS = 6
HOST = 2
REST = 4
EXT = 40
TALL = 32
BLOCKS = LON // 128

f32 = jnp.float32
bf16 = jnp.bfloat16
GRANT = pltpu.CompilerParams(vmem_limit_bytes=24 << 20)
VMEM = pl.BlockSpec(memory_space=pltpu.VMEM)
FAR = pl.BlockSpec(memory_space=pltpu.HBM)


def filter_tables():
    b = np.arange(128)[:, None].astype(np.float64)
    table = np.zeros((4, 256, 256))
    wave = np.zeros((4, 256))
    gain = np.zeros((4, 256))
    k2 = np.arange(65)[None, :]
    angle = 2 * np.pi * b * k2 / 128
    table[0, :128, :65] = np.cos(angle)
    table[0, :128, 65:128] = np.sin(angle[:, 1:64])
    wave[0, :65] = 8 * np.arange(65)
    wave[0, 65:128] = 8 * np.arange(1, 64)
    gain[0, :128] = 2.0
    gain[0, 0] = gain[0, 64] = 1.0
    k2 = np.arange(64)[None, :]
    angle = 2 * np.pi * b * (4 + 8 * k2) / 1024
    table[0, 128:, 128:192] = np.cos(angle)
    table[0, 128:, 192:] = np.sin(angle)
    wave[0, 128:192] = wave[0, 192:] = 4 + 8 * np.arange(64)
    gain[0, 128:] = 2.0
    for k1 in (1, 2, 3):
        k = k1 + 8 * np.arange(128)
        angle = 2 * np.pi * b * k[None, :] / 1024
        c, s = np.cos(angle), np.sin(angle)
        table[k1, :128, :128] = c
        table[k1, :128, 128:] = -s
        table[k1, 128:, :128] = s
        table[k1, 128:, 128:] = c
        wave[k1, :128] = wave[k1, 128:] = np.minimum(k, 1024 - k)
        gain[k1] = 2.0
    return table, wave, gain / LON


def split_value(x):
    high = x.astype(bf16)
    low = (x - high.astype(f32)).astype(bf16)
    return high, low


def dot3(a, b, dims):
    ah, al = a
    bh, bl = b

    def dot(x, y):
        return lax.dot_general(x, y, (dims, ((), ())), preferred_element_type=f32)

    return dot(ah, bh) + (dot(ah, bl) + dot(al, bh))


def turn_groups(x, sign):
    group = lax.broadcasted_iota(jnp.int32, x.shape, 2) // 16
    for d in (4, 2, 1):
        x = jnp.where((group & d) != 0, pltpu.roll(x, d if sign > 0 else 8 - d, 1), x)
    return x


def gather_rows(x):
    return pltpu.roll(turn_groups(x, -1), 0, 2, stride=COLS, stride_axis=1)


def scatter_rows(x):
    row = lax.broadcasted_iota(jnp.int32, x.shape, 1)
    for d in (4, 2, 1):
        x = jnp.where((row & d) != 0, pltpu.roll(x, 128 - COLS * d, 2), x)
    return turn_groups(x, 1)


def aligned(x):
    return pl.multiple_of(x, COLS)


def load_metric(metric, ext, sem, lat):
    start = pl.multiple_of(lat * ROWS, 8)
    low = pl.multiple_of(jnp.maximum(start - 8, 0), 8)
    high = pl.multiple_of(jnp.minimum(start + ROWS, LAT - 8), 8)
    return [
        pltpu.make_async_copy(metric.at[pl.ds(start, ROWS)], ext.at[pl.ds(8, ROWS)], sem.at[0]),
        pltpu.make_async_copy(metric.at[pl.ds(low, 8)], ext.at[pl.ds(0, 8)], sem.at[1]),
        pltpu.make_async_copy(metric.at[pl.ds(high, 8)], ext.at[pl.ds(8 + ROWS, 8)], sem.at[2]),
    ]


def mask_metric(ext, lat):
    ext[0:8, :] = ext[0:8, :] * jnp.where(lat > 0, 1.0, 0.0)
    ext[32:40, :] = ext[32:40, :] * jnp.where(lat < LAT // ROWS - 1, 1.0, 0.0)


def selection(holder):
    hb = jnp.broadcast_to(holder.astype(f32), (MODES, MODES))
    ha = hb.T
    ia = lax.broadcasted_iota(jnp.int32, (MODES, MODES), 0)
    ib = lax.broadcasted_iota(jnp.int32, (MODES, MODES), 1)
    same = jnp.where(ha == hb, 1.0, 0.0)
    before = jnp.where(ia < ib, 1.0, 0.0)
    after = jnp.where(ib < ia, 1.0, 0.0)
    rank_row = jnp.sum(same * before, axis=0, keepdims=True)
    rank_col = jnp.sum(same * after, axis=1, keepdims=True)
    over_row = jnp.where(rank_row >= HOST, 1.0, 0.0)
    over_col = jnp.where(rank_col >= HOST, 1.0, 0.0)
    over_index = jnp.sum(over_col * before, axis=0, keepdims=True)
    patch_a = (ia & (PATCHES - 1)).astype(f32)
    patch_b = (ib & (PATCHES - 1)).astype(f32)
    turn_a = (ia // PATCHES).astype(f32)
    turn_b = (ib // PATCHES).astype(f32)
    count_col = jnp.sum(jnp.where(hb == patch_a, 1.0, 0.0), axis=1, keepdims=True)
    count_row = jnp.sum(jnp.where(ha == patch_b, 1.0, 0.0), axis=0, keepdims=True)
    free_col = jnp.where(turn_a >= count_col, 1.0, 0.0)
    free_row = jnp.where(turn_b >= count_row, 1.0, 0.0)
    free_index = jnp.sum(free_row * after, axis=1, keepdims=True)
    home = jnp.where(ia.astype(f32) == rank_row * PATCHES + hb, 1.0, 0.0)
    guest = free_col * jnp.where(free_index == over_index, 1.0, 0.0)
    hosted = over_row * guest + (1.0 - over_row) * home
    rest = []
    for first in (2, 4):
        rest.append(
            jnp.where(ia.astype(f32) + first * PATCHES == rank_row * PATCHES + hb, 1.0, 0.0)
        )
    return jnp.concatenate([hosted] + rest, axis=0)


def cell_column(row):
    lane = lax.broadcasted_iota(jnp.int32, (COLS, 128), 1)
    sub = lax.broadcasted_iota(jnp.int32, (COLS, 128), 0)
    picked = jnp.where(lane == sub, jnp.broadcast_to(row, (COLS, 128)), 0.0)
    return jnp.broadcast_to(jnp.sum(picked, axis=1, keepdims=True), (COLS, 128))


def patch_kernel(
    u_far, v_far, t_far, q_far, metric, holder, project, depth, sweeps,
    packed, params, hosted, ext,
    u, v, t, q, own, field, edges, chosen, sem, field_sem,
):
    lat = lax.axis_index("lat")
    lon = lax.axis_index("lon")
    metric_copies = load_metric(metric, ext, sem, lat)
    fields = ((u_far, u), (v_far, v), (t_far, t), (q_far, q))
    copies = metric_copies + [
        pltpu.make_async_copy(far, here, field_sem.at[i]) for i, (far, here) in enumerate(fields)
    ]
    for c in copies:
        c.start()
    select = selection(holder[...])
    chosen[...] = select
    hosted[...] = select[: HOST * PATCHES].astype(bf16)
    params[...] = jnp.zeros_like(params)
    count = jnp.sum(jnp.where(holder[...] == lon, 1.0, 0.0), axis=1, keepdims=True)
    for s in range(SLOTS):
        row = chosen[pl.ds(s * PATCHES + lon, 1), :]
        value = jnp.sum(row * depth[...], axis=1, keepdims=True)
        params[0, s : s + 1, :] = jnp.broadcast_to(value, (1, 128))
        value = jnp.sum(row * sweeps[...].astype(f32), axis=1, keepdims=True)
        params[1, s : s + 1, :] = jnp.broadcast_to(value, (1, 128))
        params[2, s : s + 1, :] = jnp.broadcast_to(jnp.where(count > s, 1.0, 0.0), (1, 128))
    sel = select.astype(bf16)
    proj_high, proj_low = split_value(project[...])
    rows_high = jnp.dot(sel, proj_high, preferred_element_type=f32).astype(bf16)
    rows_low = jnp.dot(sel, proj_low, preferred_element_type=f32).astype(bf16)
    for c in metric_copies:
        c.wait()
    mask_metric(ext, lat)

    block = lon // 8
    turn = lon % 8
    offset = turn * COLS

    def lanes(b):
        return ext[:, pl.ds(pl.multiple_of(b * 128, 128), 128)]

    here = lanes(block)
    own[...] = pltpu.roll(here, (128 - offset) % 128, 1)
    west_block = jnp.where(offset == 0, (block + BLOCKS - 1) % BLOCKS, block)
    east_block = jnp.where(offset == 128 - COLS, (block + 1) % BLOCKS, block)
    west_metric = pltpu.roll(lanes(west_block), (129 - offset) % 128, 1)[8:32, 0:1]
    east_metric = pltpu.roll(lanes(east_block), (256 - COLS - offset) % 128, 1)[8:32, 0:1]
    scale = jnp.concatenate([cell_column(own[8 + r : 9 + r, :]) for r in range(ROWS)], axis=0)
    for c in copies[len(metric_copies) :]:
        c.wait()

    uu = u[...].reshape(CELLS, MODES)
    vv = v[...].reshape(CELLS, MODES)
    virtual = t[...].reshape(CELLS, MODES) * (1.0 + 0.61 * q[...].reshape(CELLS, MODES))
    eighth = 0.125 * virtual
    to_west = eighth - 0.25 * uu
    to_east = eighth + 0.25 * uu
    to_south = eighth - 0.25 * vv
    to_north = eighth + 0.25 * vv
    col = lax.broadcasted_iota(jnp.int32, (CELLS, MODES), 0) & (COLS - 1)
    around = jnp.where(col == COLS - 1, 0.0, pltpu.roll(to_west, CELLS - 1, 0))
    around = around + jnp.where(col == 0, 0.0, pltpu.roll(to_east, 1, 0))
    zero = jnp.zeros((COLS, MODES), f32)
    around = around + jnp.concatenate([to_south[COLS:], zero], axis=0)
    around = around + jnp.concatenate([zero, to_north[: CELLS - COLS]], axis=0)
    forcing = virtual + scale * (around - 0.5 * virtual)
    for r in range(ROWS):
        at = aligned(r // 8 * 128 + COLS * ((turn - r) & 7))
        field[pl.ds(at, COLS), :] = forcing[r * COLS : (r + 1) * COLS]

    edges[...] = jnp.zeros((128, MODES), f32)
    first = t[:, 0, :] * (1.0 + 0.61 * q[:, 0, :])
    last = t[:, COLS - 1, :] * (1.0 + 0.61 * q[:, COLS - 1, :])
    edge_west = jnp.broadcast_to(west_metric, (ROWS, MODES)) * (0.125 * first - 0.25 * u[:, 0, :])
    edge_east = jnp.broadcast_to(east_metric, (ROWS, MODES)) * (
        0.125 * last + 0.25 * u[:, COLS - 1, :]
    )
    for rg in range(3):
        edges[pl.ds(rg, 8, stride=COLS), :] = edge_west[8 * rg : 8 * rg + 8]
        edges[pl.ds(3 + rg, 8, stride=COLS), :] = edge_east[8 * rg : 8 * rg + 8]
    edge_south = cell_column(own[7:8, :]) * to_south[0:COLS]
    edge_north = cell_column(own[32:33, :]) * to_north[CELLS - COLS :]
    edges[8:16, :] = edge_north[0:8]
    edges[24:32, :] = edge_north[8:16]
    edges[104:112, :] = edge_south[0:8]
    edges[120:128, :] = edge_south[8:16]
    order_edges(edges, turn, field, CELLS)

    value = dot3((rows_high, rows_low), split_value(field[...]), ((1,), (1,)))
    for s in range(SLOTS):
        for part in range(4):
            packed[pl.ds(s * 4 + part, PATCHES, stride=4 * SLOTS), :] = value[
                s * PATCHES : (s + 1) * PATCHES, part * 128 : (part + 1) * 128
            ]


def order_edges(source, turn, target, base):
    sub = lax.broadcasted_iota(jnp.int32, (COLS, MODES), 0)
    for g in range(8):
        west = source[pl.ds(aligned(COLS * ((turn - 1 - g) & 7)), COLS), :]
        east = source[pl.ds(aligned(COLS * ((turn + 1 - g) & 7)), COLS), :]
        rim = source[pl.ds(aligned(COLS * ((turn - g) & 7)), COLS), :]
        target[base + COLS * g : base + COLS * g + COLS, :] = jnp.where(
            sub < 3, west, jnp.where(sub < 6, east, rim)
        )


def patch_stage(u, v, t, q, metric, holder, project, depth, sweeps):
    return pl.pallas_call(
        patch_kernel,
        name="patch_stage",

        out_shape=(
            pltpu.VMEM((PATCHES * SLOTS * 4, 128), f32),
            pltpu.VMEM((3, 8, 128), f32),
            pltpu.VMEM((HOST * PATCHES, MODES), bf16),
            pltpu.VMEM((EXT, LON), f32),
        ),
        in_specs=[FAR] * 5 + [VMEM] * 4,
        out_specs=(VMEM,) * 4,
        scratch_shapes=[pltpu.VMEM((ROWS, COLS, MODES), f32)] * 4
        + [
            pltpu.VMEM((EXT, 128), f32),
            pltpu.VMEM((CELLS + 128, MODES), f32),
            pltpu.VMEM((128, MODES), f32),
            pltpu.VMEM((SLOTS * PATCHES, MODES), f32),
            pltpu.SemaphoreType.DMA((3,)),
            pltpu.SemaphoreType.DMA((4,)),
        ],
    )(u, v, t, q, metric, holder, project, depth, sweeps)


def spread_rows(row, block, count=8):
    return pl.ds(row * BLOCKS + block, count, stride=BLOCKS)


def band_kernel(received, band, south, north):
    place = lax.broadcasted_iota(jnp.int32, (PATCHES, 128), 1) & (COLS - 1)
    near_half = (lax.broadcasted_iota(jnp.int32, (BLOCKS, 8, 128), 2) & (COLS - 1)) < 8
    row = lax.broadcasted_iota(jnp.int32, (8, 128), 0)
    for s in range(SLOTS):
        edge = received[pl.ds(s * 4 + 3, PATCHES, stride=4 * SLOTS), :]
        from_east = pltpu.roll(edge, PATCHES - 1, 0)
        from_west = pltpu.roll(edge, 1, 0)
        bands = []
        for rg in range(3):
            x = received[pl.ds(s * 4 + rg, PATCHES, stride=4 * SLOTS), :]
            x = x + jnp.where(place == COLS - 1, pltpu.roll(from_east, 15 - rg, 1), 0.0)
            x = x + jnp.where(place == 0, pltpu.roll(from_west, 128 - 3 - rg, 1), 0.0)
            bands.append(gather_rows(x.reshape(BLOCKS, 8, 128)))
        rim = gather_rows(edge.reshape(BLOCKS, 8, 128))
        low = pltpu.roll(rim, 128 - 8, 2)
        to_north = jnp.where(near_half, low, pltpu.roll(rim, 7, 1))
        to_south = jnp.where(near_half, pltpu.roll(low, 1, 1), rim)
        for b in range(BLOCKS):
            for rg in range(3):
                band[spread_rows(s * ROWS + 8 * rg, b), :] = bands[rg][b]
            south[spread_rows(s * 8, b), :] = jnp.where(row == 7, to_south[b], bands[0][b])
            north[spread_rows(s * 8, b), :] = jnp.where(row == 0, to_north[b], bands[2][b])


def band_stage(received):
    return pl.pallas_call(
        band_kernel,
        name="band_stage",

        out_shape=(
            pltpu.VMEM((SLOTS * ROWS * BLOCKS, 128), f32),
            pltpu.VMEM((SLOTS * 8 * BLOCKS, 128), f32),
            pltpu.VMEM((SLOTS * 8 * BLOCKS, 128), f32),
        ),
        in_specs=[VMEM],
        out_specs=(VMEM, VMEM, VMEM),
    )(received)


def split_eight(x, spectral, row):
    root = math.sqrt(0.5)
    s04, d04 = x[0] + x[4], x[0] - x[4]
    s26, d26 = x[2] + x[6], x[2] - x[6]
    s15, d15 = x[1] + x[5], x[1] - x[5]
    s37, d37 = x[3] + x[7], x[3] - x[7]
    even, odd = s04 + s26, s15 + s37
    lean, turn = root * (d15 - d37), root * (d15 + d37)
    at = slice(row, row + 8)
    spectral[0, at, 0:128] = even + odd
    spectral[0, at, 128:256] = even - odd
    spectral[1, at, 0:128] = d04 + lean
    spectral[1, at, 128:256] = -d26 - turn
    spectral[2, at, 0:128] = s04 - s26
    spectral[2, at, 128:256] = s37 - s15
    spectral[3, at, 0:128] = d04 - lean
    spectral[3, at, 128:256] = d26 - turn


def join_eight(spectral, row):
    root = math.sqrt(0.5)
    at = slice(row, row + 8)
    y0, y4 = spectral[0, at, 0:128], spectral[0, at, 128:256]
    p1, q1 = spectral[1, at, 0:128], spectral[1, at, 128:256]
    p2, q2 = spectral[2, at, 0:128], spectral[2, at, 128:256]
    p3, q3 = spectral[3, at, 0:128], spectral[3, at, 128:256]
    even, odd = y0 + y4, y0 - y4
    lean = root * ((p1 - p3) - (q1 + q3))
    turn = root * ((p3 - p1) - (q1 + q3))
    side, swing = p1 + p3, q3 - q1
    up, down = even + p2, even - p2
    left, right = odd - q2, odd + q2
    return (
        up + side, left + lean, down + swing, right + turn,
        up - side, left - lean, down - swing, right - turn,
    )


def solve_slots(
    first, count, edge, band, rims, from_south, from_north, params, metric, damping,
    fetches, constants, totals, spectral, solved,
):
    table_high, table_low, back_high, back_low = constants
    height = solved.shape[1]
    reach = MAXIT - 1 + edge
    out = ROWS + 2 * edge

    def rows_list(x):
        return [x[r : r + 1] for r in range(x.shape[0])]

    def neighbours(x):
        lane = lax.broadcasted_iota(jnp.int32, x.shape, 2)
        east = pltpu.roll(x, 127, 2)
        east = jnp.where(lane == 127, pltpu.roll(east, BLOCKS - 1, 1), east)
        west = pltpu.roll(x, 1, 2)
        west = jnp.where(lane == 0, pltpu.roll(west, 1, 1), west)
        return east + west

    for i in range(count):
        s = first + i
        depth = params[0, s : s + 1, 0:1]
        number = params[1, s : s + 1, 0:1]
        depth = jnp.where(depth > 0.0, depth, 1.0)
        centre = 1.0 + 8.0 * depth
        radius = 8.0 * depth
        relative = centre / radius
        ratio = 1.0 / relative

        def wide(x):
            return jnp.broadcast_to(x, (BLOCKS, 128))[None]


        def rows_of(source, rows):
            x = source[s * rows * BLOCKS : (s + 1) * rows * BLOCKS, :]
            return x.reshape(rows, BLOCKS, 128)

        below, above, mine = rows_of(from_south, 8), rows_of(from_north, 8), rows_of(band, ROWS)
        residual = jnp.concatenate(
            [
                below[8 - reach : 7],
                below[7:8] + rows_of(rims, 2)[0:1],
                mine[0:1] + below[0:1],
                mine[1:23],
                mine[23:24] + above[7:8],
                above[0:1] + rows_of(rims, 2)[1:2],
                above[1:reach],
            ],
            axis=0,
        )
        height_now = ROWS + 2 * reach - 2
        at = (8 - reach + 1) * BLOCKS
        coupling = wide(depth) * metric[at : at + height_now * BLOCKS, :].reshape(
            height_now, BLOCKS, 128
        )
        direction = residual * wide(1.0 / centre)
        total = rows_list(direction[MAXIT - 1 : MAXIT - 1 + out])
        direction, residual, coupling = map(rows_list, (direction, residual, coupling))
        for sweep in range(1, MAXIT):
            after = 1.0 / (2.0 * relative - ratio)
            keep, push = wide(after * ratio), wide(2.0 * after / radius)
            active = wide(jnp.where(number > sweep, 1.0, 0.0))
            ratio = after
            low = MAXIT - 1 - sweep
            fresh, left = [], []
            for r in range(len(direction) - 2):
                middle = direction[r + 1]
                around = neighbours(middle) + (direction[r] + direction[r + 2])
                rest = residual[r + 1] - middle + coupling[r + sweep - 1] * (around - 4.0 * middle)
                left.append(rest)
                fresh.append(keep * middle + push * rest)
                if low <= r < low + out:
                    gain = fresh[r] if sweep < MINIT else active * fresh[r]
                    total[r - low] = total[r - low] + gain
            direction, residual = fresh, left
        total = jnp.concatenate(total, axis=0)
        at = i * height * BLOCKS
        if edge:
            parts = [total[1 : ROWS + 2], total[0:1]]
            parts.append(jnp.zeros((height - ROWS - 2, BLOCKS, 128), f32))
            total = jnp.concatenate(parts, axis=0)
        totals[at : at + height * BLOCKS, :] = total.reshape(height * BLOCKS, 128)
        for row in range(i * height, (i + 1) * height, 8):
            split_eight([totals[spread_rows(row, a), :] for a in range(BLOCKS)], spectral, row)
    for c in fetches[:2]:
        c.wait()
    for k in range(4):
        table = (table_high[k], table_low[k])
        weight = jnp.concatenate([damping[k, 0:height, :]] * count, axis=0)
        spectrum = dot3(split_value(spectral[k, 0 : count * height, :]), table, ((1,), (0,)))
        if k == 0:
            for c in fetches[2:]:
                c.wait()
        back = (back_high[k], back_low[k])
        spectral[k, 0 : count * height, :] = dot3(split_value(spectrum * weight), back, ((1,), (0,)))
    for row in range(0, count * height, 8):
        i, start = row // height, row % height
        for a, part in enumerate(join_eight(spectral, row)):
            solved[i, start : start + 8, 128 * a : 128 * a + 128] = part


def damping_kernel(ext, south, north, cutoff, wave, gain, damping, metric, rims):
    for s in range(SLOTS):
        top, bottom = s * 8 * BLOCKS, 2 * s * BLOCKS
        rims[bottom : bottom + BLOCKS, :] = south[top + 7 * BLOCKS : top + 8 * BLOCKS, :]
        rims[bottom + BLOCKS : bottom + 2 * BLOCKS, :] = north[top : top + BLOCKS, :]
    for tile in range(EXT // 8):
        for b in range(BLOCKS):
            metric[spread_rows(8 * tile, b), :] = ext[
                8 * tile : 8 * tile + 8, 128 * b : 128 * b + 128
            ]
    start = lax.axis_index("lat") * ROWS
    sub = lax.broadcasted_iota(jnp.int32, (TALL, 128), 0)
    index = jnp.where(sub == ROWS + 1, start - 1, start + sub)
    lane = lax.broadcasted_iota(jnp.int32, (TALL, 128), 1)
    limit = jnp.zeros((TALL, 1), f32)
    for b in range(LAT // 128):
        picked = jnp.where(
            lane + 128 * b == index, jnp.broadcast_to(cutoff[b : b + 1, :], (TALL, 128)), 0.0
        )
        limit = limit + jnp.sum(picked, axis=1, keepdims=True)
    limit = jnp.where(limit > 0.0, limit, 1.0)
    inverse = jnp.broadcast_to(1.0 / (limit * (0.5 * LON)), (TALL, 256))
    for k in range(4):
        ratio = jnp.broadcast_to(wave[k : k + 1, :], (TALL, 256)) * inverse
        ratio = ratio * ratio
        damping[k] = jnp.broadcast_to(gain[k : k + 1, :], (TALL, 256)) / (1.0 + ratio * ratio)


def damping_stage(*operands):
    return pl.pallas_call(
        damping_kernel,
        name="damping_stage",
        out_shape=(
            pltpu.VMEM((4, TALL, 256), f32),
            pltpu.VMEM((EXT * BLOCKS, 128), f32),
            pltpu.VMEM((SLOTS * 2 * BLOCKS, 128), f32),
        ),
        in_specs=[VMEM] * 6,
        out_specs=(VMEM,) * 3,
    )(*operands)


def fetch_all(far, here, sem):
    fetches = [
        pltpu.make_async_copy(source, target, sem.at[i])
        for i, (source, target) in enumerate(zip(far, here))
    ]
    for c in fetches:
        c.start()
    return fetches


def host_kernel(
    band, rims, from_south, from_north, params, metric, damping,
    *rest,
):
    far_constants, (packed, own_modes, totals, spectral, solved), (*constants, sem) = (
        rest[:4], rest[4:9], rest[9:],
    )
    fetches = fetch_all(far_constants, constants, sem)
    solve_slots(
        0, HOST, 1, band, rims, from_south, from_north, params, metric, damping, fetches,
        constants, totals, spectral, solved,
    )
    place = lax.broadcasted_iota(jnp.int32, (PATCHES, 128), 1) & (COLS - 1)
    row = lax.broadcasted_iota(jnp.int32, (BLOCKS, 8, 128), 1)
    for i in range(HOST):
        owned = jnp.broadcast_to(params[2, i : i + 1, 0:1], (ROWS, LON))
        own_modes[i] = solved[i, 0:ROWS, :] * owned

        def tile(k):
            return jnp.stack(
                [solved[i, 8 * k : 8 * k + 8, 128 * b : 128 * b + 128] for b in range(BLOCKS)]
            )

        last = tile(3)
        shifted = pltpu.roll(last, 8, 2)
        rim = jnp.where(
            row == 0,
            shifted,
            jnp.where(
                row == 1,
                pltpu.roll(last, 1, 1),
                jnp.where(row == 6, pltpu.roll(shifted, 5, 1), pltpu.roll(last, 6, 1)),
            ),
        )
        edge = scatter_rows(rim).reshape(PATCHES, 128)
        for rg in range(3):
            x = scatter_rows(tile(rg)).reshape(PATCHES, 128)
            packed[pl.ds(i * 4 + rg, PATCHES, stride=4 * HOST), :] = x
            west = pltpu.roll(pltpu.roll(x, 1, 0), 128 - 15 + rg, 1)
            east = pltpu.roll(pltpu.roll(x, PATCHES - 1, 0), 3 + rg, 1)
            edge = jnp.where(place == rg, west, edge)
            edge = jnp.where(place == 3 + rg, east, edge)
        packed[pl.ds(i * 4 + 3, PATCHES, stride=4 * HOST), :] = edge


def solver_scratch(count, height):
    return [
        pltpu.VMEM((count * height * BLOCKS, 128), f32),
        pltpu.VMEM((4, count * height, 256), f32),
        pltpu.VMEM((count, height, LON), f32),
        pltpu.VMEM((4, 256, 256), bf16),
        pltpu.VMEM((4, 256, 256), bf16),
        pltpu.VMEM((4, 256, 256), bf16),
        pltpu.VMEM((4, 256, 256), bf16),
        pltpu.SemaphoreType.DMA((4,)),
    ]


def host_stage(*operands):
    return pl.pallas_call(
        host_kernel,
        name="host_stage",

        out_shape=(
            pltpu.VMEM((PATCHES * HOST * 4, 128), f32),
            pltpu.VMEM((HOST, ROWS, LON), f32),
        ),
        in_specs=[VMEM] * 7 + [FAR] * 4,
        out_specs=(VMEM, VMEM),
        scratch_shapes=solver_scratch(HOST, TALL),
    )(*operands)


def rest_kernel(
    band, rims, from_south, from_north, params, metric, damping,
    *rest,
):
    far_constants, rest = rest[:4], rest[4:]
    own_modes, hosted, expand, u_far, v_far, modes, expand_high, expand_low, u, v = rest[:10]
    cell_metric, totals, spectral, solved, *constants, sem, wind_sem, own = rest[10:]
    winds = fetch_all((u_far, v_far), (u, v), wind_sem)
    fetches = fetch_all(far_constants, constants, sem)
    high, low = split_value(expand[...])
    dims = (((1,), (1,)), ((), ()))
    expand_high[...] = lax.dot_general(
        hosted[...], high, dims, preferred_element_type=f32
    ).astype(bf16)
    expand_low[...] = lax.dot_general(
        hosted[...], low, dims, preferred_element_type=f32
    ).astype(bf16)
    modes[0:HOST] = own_modes[...]
    solve_slots(
        HOST, REST, 0, band, rims, from_south, from_north, params, metric, damping, fetches,
        constants, totals, spectral, solved,
    )
    for i in range(REST):
        modes[HOST + i] = solved[i]
    lon = lax.axis_index("lon")
    own[...] = pltpu.roll(
        metric[spread_rows(8, lon // 8, ROWS), :], (128 - lon % 8 * COLS) % 128, 1
    )
    for r in range(ROWS):
        cell_metric[r * COLS : (r + 1) * COLS, :] = 0.25 * cell_column(own[r : r + 1, :])
    for c in winds:
        c.wait()


def rest_stage(*operands):
    return pl.pallas_call(
        rest_kernel,
        name="rest_stage",

        out_shape=(
            jax.ShapeDtypeStruct((SLOTS, ROWS, LON), f32),
            pltpu.VMEM((MODES, MODES), bf16),
            pltpu.VMEM((MODES, MODES), bf16),
            pltpu.VMEM((ROWS, COLS, MODES), f32),
            pltpu.VMEM((ROWS, COLS, MODES), f32),
            pltpu.VMEM((CELLS, MODES), f32),
        ),
        in_specs=[VMEM] * 7 + [FAR] * 4 + [VMEM] * 3 + [FAR] * 2,
        out_specs=(VMEM,) * 6,
        scratch_shapes=solver_scratch(REST, ROWS)
        + [pltpu.SemaphoreType.DMA((2,)), pltpu.VMEM((ROWS, 128), f32)],
    )(*operands)


def wind_kernel(
    received, expand_high, expand_low, cell_metric, u, v, u_new, v_new, tall, edges, edge
):
    turn = lax.axis_index("lon") % 8
    table = (expand_high[...], expand_low[...])
    for part in range(4):
        x = jnp.concatenate(
            [received[pl.ds(i * 4 + part, PATCHES, stride=4 * HOST), :] for i in range(HOST)],
            axis=0,
        )
        value = dot3(split_value(x.T), table, ((1,), (0,)))
        if part < 3:
            for g in range(8):
                at = aligned(COLS + part * 128 + COLS * ((turn - g) & 7))
                tall[pl.ds(at, COLS), :] = value[COLS * g : COLS * g + COLS]
        else:
            edges[...] = value
    order_edges(edges, turn, edge, 0)
    tall[0:8, :] = edge[104:112, :]
    tall[8:16, :] = edge[120:128, :]
    tall[CELLS + COLS : CELLS + COLS + 8, :] = edge[8:16, :]
    tall[CELLS + COLS + 8 : CELLS + 2 * COLS, :] = edge[24:32, :]
    pressure = tall[COLS : CELLS + COLS, :]

    def spread(base):
        return jnp.concatenate(
            [
                jnp.broadcast_to(
                    edge[(r % 8) * COLS + base + r // 8 : (r % 8) * COLS + base + r // 8 + 1, :],
                    (COLS, MODES),
                )
                for r in range(ROWS)
            ],
            axis=0,
        )

    col = lax.broadcasted_iota(jnp.int32, (CELLS, MODES), 0) & (COLS - 1)
    east = jnp.where(col == COLS - 1, spread(3), pltpu.roll(pressure, CELLS - 1, 0))
    west = jnp.where(col == 0, spread(0), pltpu.roll(pressure, 1, 0))
    scale = cell_metric[...]
    u_new[...] = u[...] - (scale * (east - west)).reshape(ROWS, COLS, MODES)
    slope = tall[2 * COLS : CELLS + 2 * COLS, :] - tall[0:CELLS, :]
    v_new[...] = v[...] - (scale * slope).reshape(ROWS, COLS, MODES)


def wind_stage(*operands):
    shape = jax.ShapeDtypeStruct((ROWS, COLS, MODES), f32)
    return pl.pallas_call(
        wind_kernel,
        name="wind_stage",

        out_shape=(shape, shape),
        in_specs=[VMEM] * 6,
        out_specs=(VMEM, VMEM),
        scratch_shapes=[
            pltpu.VMEM((CELLS + 2 * COLS, MODES), f32),
            pltpu.VMEM((128, MODES), f32),
            pltpu.VMEM((128, MODES), f32),
        ],
    )(*operands)


def near(*arrays):
    return tuple(pltpu.with_memory_space_constraint(x, pltpu.VMEM) for x in arrays)


def exchange(x, rows):
    x = x.reshape(PATCHES, rows, 128)
    x = lax.all_to_all(x, "lon", split_axis=0, concat_axis=0, tiled=True)
    return x.reshape(PATCHES * rows, 128)


def local(
    eastward_velocity,
    northward_velocity,
    thermal_anomaly,
    water_content,
    gridbox_factor,
    filter_threshold,
    layers_to_eigen,
    eigen_to_layers,
    eigen_screening_factor,
    chebyshev_sweeps,
    eigen_region_holder,
):
    table, wave, gain = filter_tables()
    tables = []
    for x in (table, table.transpose(0, 2, 1)):
        high = np.asarray(x, np.float32).astype(bf16)
        tables += [high, (x - high.astype(np.float64)).astype(np.float32).astype(bf16)]
    constants = [jnp.asarray(x) for x in [wave.astype(np.float32), gain.astype(np.float32)] + tables]
    packed, params, hosted, ext = patch_stage(
        eastward_velocity,
        northward_velocity,
        thermal_anomaly,
        water_content,
        gridbox_factor,
        eigen_region_holder.reshape(1, MODES),
        layers_to_eigen,
        eigen_screening_factor.reshape(1, MODES),
        chebyshev_sweeps.reshape(1, MODES),
    )
    wave, gain, *constants = constants

    band, south, north = band_stage(*near(exchange(packed, 4 * SLOTS)))
    size = lax.axis_size("lat")
    up = [(i, i + 1) for i in range(size - 1)]
    down = [(j, i) for i, j in up]
    from_south = lax.ppermute(north, "lat", up)
    from_north = lax.ppermute(south, "lat", down)
    damping, metric, rims = damping_stage(
        *near(ext, south, north), filter_threshold.reshape(LAT // 128, 128), wave, gain
    )
    solver = near(band, rims, from_south, from_north, params, metric, damping) + tuple(
        constants
    )
    returned, own_modes = host_stage(*solver)
    returned = exchange(returned, 4 * HOST)
    mode_solution, expand_high, expand_low, u, v, cell_metric = rest_stage(
        *solver, *near(own_modes, hosted), eigen_to_layers, eastward_velocity, northward_velocity
    )
    u_new, v_new = wind_stage(
        *near(returned, expand_high, expand_low, cell_metric, u, v)
    )
    return u_new, v_new, mode_solution


def solution(mesh):
    return jax.shard_map(
        local,
        mesh=mesh,
        in_specs=(P("lat", "lon", None),) * 4 + (P(),) * 7,
        out_specs=(P("lat", "lon", None), P("lat", "lon", None), P("lon", "lat", None)),
        check_vma=False,
    )
```
